512 devices in a mesh: gx: 64 (over y, x, core), gz: 8 (over z).
Axes of the slice: x: 4, y: 8, z: 8, core: 2. Of those that a mesh axis runs over, the one named last changes fastest.
Arguments:
- velocity: bfloat16 [3, 32, 512, 64, 128], P(None, None, 'gx', 'gz'), may hold values from -16 to 16
- weights: float32 [512, 64, 128], P('gx', 'gz'), may hold values from 1 to 60
Outputs:
- modes: float32 [3, 32, 512, 64, 128], P(None, None, 'gx', 'gz')
The draws below stay inside these ranges and needn't reach their ends.
All inputs are finite; a program needn't handle non-finite values.
Results may differ from the reference program's by a relative error of at most 0.0003.
Values may be sent and summed in bfloat16 or wider, within the bound.
A program may use at most 64 MiB of HBM per device.

```python
import jax
import jax.numpy as jnp
from jax import lax

SNAP = 32
CX = 8
NY = 128
NX = 512
NZ = 64


def draw_velocity(key, part):
    keys = jax.random.split(key, 4)
    common = jax.random.normal(keys[0], (3, 1, NX, NZ, NY), jnp.float32)
    own = jax.random.normal(keys[1], (3, SNAP, NX, NZ, NY), jnp.float32)
    coefs = jax.random.uniform(keys[2], (1, SNAP, 1, 1, 1), jnp.float32, 0.5, 1.5)
    spread = jax.random.uniform(keys[3], (1, SNAP, 1, 1, 1), jnp.float32, 0.0, 1.0)
    scales = jnp.exp(jnp.log(4.0) * spread / jnp.max(spread))
    field = scales * jnp.clip(coefs * common + 0.8 * own, -4.0, 4.0)
    return field.astype(jnp.bfloat16)


def draw_weights(key, part):
    stream = jnp.arange(NX, dtype=jnp.float32)[:, None, None] / (NX - 1)
    span = jnp.arange(NZ, dtype=jnp.float32)[None, :, None] / (NZ - 1)
    rising = (1.0 + 2.0 * stream) * (1.0 + span)
    base = jnp.exp(jax.random.uniform(key, (NX, NZ, NY), jnp.float32, jnp.log(0.8), jnp.log(12.0)))
    return (rising * jnp.clip(base, 1.0, 10.0)).astype(jnp.float32)


def setup_inputs(seed: int = 0) -> dict:
    arg_keys = jax.random.split(jax.random.key(seed), 3)
    velocity = draw_velocity(jax.random.fold_in(arg_keys[2], 71), 0)
    weights = draw_weights(jax.random.fold_in(arg_keys[2], 71), 0)
    return dict(velocity=velocity, weights=weights)


COEFS = (0.8, -0.2, 4.0 / 105.0, -1.0 / 280.0)

def taps(extended, axis, length):
    total = None
    for step, weight in enumerate(COEFS, start=1):
        upper = lax.slice_in_dim(extended, 4 + step, 4 + step + length, axis=axis)
        lower = lax.slice_in_dim(extended, 4 - step, 4 - step + length, axis=axis)
        term = weight * (upper - lower)
        total = term if total is None else total + term
    return total

def rolled(field, axis):
    total = None
    for step, weight in enumerate(COEFS, start=1):
        term = weight * (jnp.roll(field, -step, axis) - jnp.roll(field, step, axis))
        total = term if total is None else total + term
    return total

def walled(field):
    padded = jnp.pad(field, ((0, 0), (0, 0), (0, 0), (4, 4)))
    return taps(padded, 3, field.shape[3])

def block_vorticity(velocity, block):
    index = ((block * CX - 4 + jnp.arange(CX + 8, dtype=jnp.int32)) % NX).astype(jnp.int32)
    extended = jnp.take(velocity, index, axis=2).astype(jnp.float32)
    inner = extended[:, :, 4:4 + CX]
    omega_x = walled(inner[2]) - rolled(inner[1], 2)
    omega_y = rolled(inner[0], 2) - taps(extended[2], 1, CX)
    omega_z = taps(extended[1], 1, CX) - walled(inner[0])
    return jnp.stack([omega_x, omega_y, omega_z])

def reference(velocity, weights):
    blocks = NX // CX

    def add_block(block, gram):
        vort = block_vorticity(velocity, block)
        local_w = lax.dynamic_slice_in_dim(weights, (block * CX).astype(jnp.int32), CX, 0)
        term = lax.dot_general((vort * local_w[None, None]).astype(jnp.float32), vort.astype(jnp.float32), (((0, 2, 3, 4), (0, 2, 3, 4)), ((), ())), precision=lax.Precision.HIGHEST, preferred_element_type=jnp.float32)
        return gram + term
    gram = lax.fori_loop(0, blocks, add_block, jnp.zeros((SNAP, SNAP), jnp.float32))
    factor = jnp.linalg.cholesky(gram)
    inverse = jax.scipy.linalg.solve_triangular(factor, jnp.eye(SNAP, dtype=jnp.float32), lower=True)
    scale_all = jnp.sqrt(jnp.float32(3 * NX * NY * NZ))

    def write_block(block, modes):
        vort = block_vorticity(velocity, block)
        mixed = jnp.einsum('ij,cjxzy->cixzy', inverse, vort, precision=lax.Precision.HIGHEST)
        return lax.dynamic_update_slice_in_dim(modes, mixed * scale_all, (block * CX).astype(jnp.int32), 2)
    return lax.fori_loop(0, blocks, write_block, jnp.zeros((3, SNAP, NX, NZ, NY), jnp.float32))
```

```python
import functools

import jax
import jax.numpy as jnp
from jax import lax
from jax.experimental import pallas as pl
from jax.experimental.pallas import tpu as pltpu
from jax.sharding import PartitionSpec as P

COEFS = (0.8, -0.2, 4.0 / 105.0, -1.0 / 280.0)
MESH = pl.DeviceIdType.MESH
F32 = jnp.float32
BF16 = jnp.bfloat16
PAIR = 2
CHUNKS = 4
U, V, W = 0, 1, 2


def groups_of(count):
    low = 8 if count % 8 == 0 else 2
    return low, count // low


def dot_nt(a, b):
    return lax.dot_general(a, b, (((1,), (1,)), ((), ())), preferred_element_type=F32)


def dot_nn(a, b):
    return lax.dot_general(a, b, (((1,), (0,)), ((), ())), preferred_element_type=F32)


def combine(upper_of, lower_of):
    total = None
    for step, weight in enumerate(COEFS, start=1):
        term = weight * (upper_of(step) - lower_of(step))
        total = term if total is None else total + term
    return total


def along_lanes(field):
    rows, lanes = field.shape
    lane = lax.broadcasted_iota(jnp.int32, (rows, lanes), 1)

    def upper(step):
        return jnp.where(lane < lanes - step, pltpu.roll(field, lanes - step, 1), 0.0)

    def lower(step):
        return jnp.where(lane >= step, pltpu.roll(field, step, 1), 0.0)

    return combine(upper, lower)


def along_sublanes(inner, halo):
    count, cells, lanes = inner.shape
    row = lax.broadcasted_iota(jnp.int32, (count, cells, lanes), 1)

    def upper(step):
        return pltpu.roll(jnp.where(row < step, halo, inner), cells - step, 1)

    def lower(step):
        return pltpu.roll(jnp.where(row >= cells - step, halo, inner), step, 1)

    return combine(upper, lower)


def gram_kernel(
    axes,
    vel_hbm,
    weights_ref,
    gram_ref,
    high_hbm,
    low_hbm,
    vel,
    halo_x,
    halo_z,
    part,
    high,
    low,
    acc,
    slots,
    vel_sem,
    x_send,
    x_recv,
    z_send,
    z_recv,
    slot_send,
    slot_recv,
    out_sem,
):
    snaps, cells_x, cells_z, cells_y = vel_hbm.shape[1:]
    count_x, count_z = axes
    low_count, high_count = groups_of(count_x)
    gx, gz = lax.axis_index("gx"), lax.axis_index("gz")
    near, far = lax.rem(gx, low_count), gx // low_count
    right_x, left_x = lax.rem(gx + 1, count_x), lax.rem(gx + count_x - 1, count_x)
    right_z, left_z = lax.rem(gz + 1, count_z), lax.rem(gz + count_z - 1, count_z)
    width = 4

    loads = [
        pltpu.make_async_copy(vel_hbm.at[c], vel.at[c], vel_sem.at[c]) for c in range(3)
    ]
    for load in loads:
        load.start()

    phases = (
        (count_z, gz, lambda q: (gx, q)),
        (low_count, near, lambda q: (far * low_count + q, gz)),
        (high_count, far, lambda q: (q * low_count + near, gz)),
    )

    barrier = pltpu.get_barrier_semaphore()
    total_signals = 2
    for peer in ((right_x, gz), (left_x, gz)):
        pl.semaphore_signal(barrier, inc=1, device_id=peer, device_id_type=MESH)
    for count, place, peer_of in phases:
        for d in range(1, count):
            pl.semaphore_signal(
                barrier, inc=1, device_id=peer_of(lax.rem(place + d, count)), device_id_type=MESH
            )
            total_signals += 1
    pl.semaphore_wait(barrier, total_signals)

    planes = cells_x // CHUNKS
    z_copies = {}
    x_copies = {}

    def start_z(k):
        source = (V, U)[k]
        for chunk in range(CHUNKS):
            xs = pl.ds(chunk * planes, planes)
            for side, peer in ((0, (gx, left_z)), (1, (gx, right_z))):
                rows = pl.ds(side * width, width)
                copy = pltpu.make_async_remote_copy(
                    src_ref=vel_hbm.at[source, :, xs, rows, :],
                    dst_ref=halo_z.at[k, :, xs, rows, :],
                    send_sem=z_send.at[k, chunk, side],
                    recv_sem=z_recv.at[k, chunk, side],
                    device_id=peer,
                    device_id_type=MESH,
                )
                copy.start()
                z_copies[k, chunk, side] = copy

    def start_x():
        for k, source in enumerate((V, W)):
            for side, peer, first in ((0, (right_x, gz), cells_x - width), (1, (left_x, gz), 0)):
                copy = pltpu.make_async_remote_copy(
                    src_ref=vel_hbm.at[source, :, pl.ds(first, width)],
                    dst_ref=halo_x.at[k, side],
                    send_sem=x_send.at[k, side],
                    recv_sem=x_recv.at[k, side],
                    device_id=peer,
                    device_id_type=MESH,
                )
                copy.start()
                x_copies[k, side] = copy

    start_x()
    start_z(0)
    start_z(1)

    for load in loads:
        load.wait()

    rows_pair = PAIR * cells_z

    @pl.loop(0, snaps)
    def _(s):
        for k, source in enumerate((W, U)):
            field = vel[source, s].astype(F32).reshape(cells_x * cells_z, cells_y)
            part[k, s] = along_lanes(field).reshape(cells_x, cells_z, cells_y)

    root = jnp.sqrt(weights_ref[...])

    def keep(c, i, first, value):
        for x in range(value.shape[1]):
            scaled = (value[:, x] * root[first + x][None]).reshape(rows_pair, cells_y)
            rounded = scaled.astype(BF16)
            rows = pl.ds(pl.multiple_of(i * rows_pair, rows_pair), rows_pair)
            high[c, first + x, rows, :] = rounded
            low[c, first + x, rows, :] = (scaled - rounded.astype(F32)).astype(BF16)

    def accumulate(c, first, count):
        tops = [high[c, first + x] for x in range(count)]
        rests = [low[c, first + x] for x in range(count)]
        left = jnp.concatenate(tops + tops + rests, axis=1)
        right = jnp.concatenate(tops + rests + tops, axis=1)
        acc[...] += dot_nt(left, right)

    acc[...] = jnp.zeros_like(acc)

    def stream(k, pair):
        ext = jnp.concatenate(
            [
                halo_x[k, 0, pair].astype(F32),
                vel[(V, W)[k], pair].astype(F32),
                halo_x[k, 1, pair].astype(F32),
            ],
            axis=1,
        )
        return combine(
            lambda step: ext[:, width + step : width + step + cells_x],
            lambda step: ext[:, width - step : width - step + cells_x],
        )

    for side in range(2):
        x_copies[0, side].wait_recv()

    @pl.loop(0, snaps // PAIR)
    def _(i):
        pair = pl.ds(i * PAIR, PAIR)
        keep(2, i, 0, stream(0, pair) - part[1, pair])

    for side in range(2):
        x_copies[1, side].wait_recv()

    @pl.loop(0, snaps // PAIR)
    def _(i):
        pair = pl.ds(i * PAIR, PAIR)
        part[1, pair] = stream(1, pair)

    for chunk in range(CHUNKS):
        accumulate(2, chunk * planes, planes)

    outs = []

    def send_out(c):
        for n, (source, target) in enumerate(((high, high_hbm), (low, low_hbm))):
            copy = pltpu.make_async_copy(source.at[c], target.at[c], out_sem.at[n, c])
            copy.start()
            outs.append(copy)

    send_out(2)

    for k, source in enumerate((V, U)):
        for chunk in range(CHUNKS):
            first = chunk * planes
            xs = pl.ds(first, planes)
            for side in range(2):
                z_copies[k, chunk, side].wait_recv()

            @pl.loop(0, snaps // PAIR)
            def _(i):
                pair = pl.ds(i * PAIR, PAIR)
                inner = vel[source, pair, xs].astype(F32)
                beside = halo_z[k, pair, xs].astype(F32)
                shape = inner.shape
                flat = (PAIR * planes, cells_z, cells_y)
                span = along_sublanes(inner.reshape(flat), beside.reshape(flat)).reshape(shape)
                other = part[k, pair, xs]
                keep(k, i, first, other - span if k == 0 else span - other)

            accumulate(k, first, planes)
        send_out(k)

    size = snaps * cells_z
    square = acc[...].reshape(snaps, cells_z, size)
    row = lax.broadcasted_iota(jnp.int32, square.shape, 1)
    column = lax.broadcasted_iota(jnp.int32, square.shape, 2)
    matched = jnp.where(row == lax.rem(column, cells_z), square, 0.0).sum(axis=1)
    lanes = gram_ref.shape[1]
    place_row = lax.broadcasted_iota(jnp.int32, (size, lanes), 0)
    place_col = lax.broadcasted_iota(jnp.int32, (size, lanes), 1)
    packed = None
    per_row = gram_ref.shape[0]
    for q in range(snaps // per_row):
        gather = (place_row // cells_z + q * snaps == place_col).astype(BF16)
        piece = matched[q * per_row : (q + 1) * per_row]
        one = piece.astype(BF16)
        rest = piece - one.astype(F32)
        two = rest.astype(BF16)
        three = (rest - two.astype(F32)).astype(BF16)
        term = dot_nn(one, gather) + dot_nn(two, gather) + dot_nn(three, gather)
        packed = term if packed is None else packed + term

    slot_copies = []
    value = packed
    for phase, (count, place, peer_of) in enumerate(phases):
        slots[phase, place] = value
        waits = []
        for d in range(1, count):
            q = lax.rem(place + d, count)
            copy = pltpu.make_async_remote_copy(
                src_ref=slots.at[phase, place],
                dst_ref=slots.at[phase, place],
                send_sem=slot_send.at[phase, d],
                recv_sem=slot_recv.at[phase, place],
                device_id=peer_of(q),
                device_id_type=MESH,
            )
            copy.start()
            slot_copies.append(copy)
            waits.append(
                pltpu.make_async_remote_copy(
                    src_ref=slots.at[phase, q],
                    dst_ref=slots.at[phase, q],
                    send_sem=slot_send.at[phase, d],
                    recv_sem=slot_recv.at[phase, q],
                    device_id=peer_of(q),
                    device_id_type=MESH,
                )
            )
        for copy in waits:
            copy.wait_recv()
        terms = [slots[phase, j] for j in range(count)]
        while len(terms) > 1:
            terms = [sum(terms[j + 1 : j + 2], terms[j]) for j in range(0, len(terms), 2)]
        value = terms[0]
    gram_ref[...] = value

    for copy in slot_copies:
        copy.wait_send()
    for copy in x_copies.values():
        copy.wait_send()
    for copy in z_copies.values():
        copy.wait_send()
    for copy in outs:
        copy.wait()


def gram_call(axes, velocity, weights):
    _, snaps, cells_x, cells_z, cells_y = velocity.shape
    size = snaps * cells_z
    held = jax.ShapeDtypeStruct((3, cells_x, size, cells_y), BF16)
    dma = pltpu.SemaphoreType.DMA
    most = 8
    return pl.pallas_call(
        functools.partial(gram_kernel, axes),
        out_shape=(jax.ShapeDtypeStruct((8, 128), F32), held, held),
        in_specs=[
            pl.BlockSpec(memory_space=pl.ANY),
            pl.BlockSpec(memory_space=pltpu.VMEM),
        ],
        out_specs=(
            pl.BlockSpec(memory_space=pltpu.VMEM),
            pl.BlockSpec(memory_space=pl.ANY),
            pl.BlockSpec(memory_space=pl.ANY),
        ),
        scratch_shapes=[
            pltpu.VMEM(velocity.shape, BF16),
            pltpu.VMEM((2, 2, snaps, 4, cells_z, cells_y), BF16),
            pltpu.VMEM((2, snaps, cells_x, cells_z, cells_y), BF16),
            pltpu.VMEM((2, snaps, cells_x, cells_z, cells_y), F32),
            pltpu.VMEM(held.shape, BF16),
            pltpu.VMEM(held.shape, BF16),
            pltpu.VMEM((size, size), F32),
            pltpu.VMEM((3, most, 8, 128), F32),
            dma((3,)),
            dma((2, 2)),
            dma((2, 2)),
            dma((2, CHUNKS, 2)),
            dma((2, CHUNKS, 2)),
            dma((3, most)),
            dma((3, most)),
            dma((2, 3)),
        ],
        compiler_params=pltpu.CompilerParams(
            collective_id=0, has_side_effects=True, vmem_limit_bytes=28 << 20
        ),
        name="curl_gram",
    )(velocity, weights)


def mix_kernel(
    scale, gram_ref, weights_ref, high_hbm, low_hbm, out_hbm, high, low, out, in_sem, out_sem
):
    _, cells_x, size, cells_y = high.shape
    snaps = out.shape[1]
    cells_z = size // snaps
    loads = []
    for c in range(3):
        for n, (source, target) in enumerate(((high_hbm, high), (low_hbm, low))):
            copy = pltpu.make_async_copy(source.at[c], target.at[c], in_sem.at[n, c])
            copy.start()
            loads.append(copy)

    packed = gram_ref[...]
    lanes = packed.shape[1]
    lane = lax.broadcasted_iota(jnp.int32, (snaps, lanes), 1)
    row = lax.broadcasted_iota(jnp.int32, (snaps, lanes), 0)
    pieces = [packed] + [
        pltpu.roll(packed, lanes - q * snaps, 1) for q in range(1, lanes // snaps)
    ]
    work = jnp.concatenate(pieces, axis=0)
    work = jnp.where(lane < snaps, work, jnp.where(lane == row + snaps, 1.0, 0.0))
    for k in range(snaps - 1):
        pivot = work[k : k + 1]
        column = work[:, k : k + 1] / work[k : k + 1, k : k + 1]
        work = work - jnp.where(row > k, column, 0.0) * pivot
    diagonal = jnp.where(lane == row, work, 0.0).sum(axis=1, keepdims=True)
    work = jnp.where((lane >= snaps) & (lane < 2 * snaps), work, 0.0) / jnp.sqrt(diagonal)

    spread_row = lax.broadcasted_iota(jnp.int32, (lanes, size), 0)
    spread_col = lax.broadcasted_iota(jnp.int32, (lanes, size), 1)
    spread = (spread_row == snaps + spread_col // cells_z).astype(BF16)
    top = work.astype(BF16)
    rest = (work - top.astype(F32)).astype(BF16)
    cube = (snaps, cells_z, size)
    match = lax.broadcasted_iota(jnp.int32, cube, 1) == lax.rem(
        lax.broadcasted_iota(jnp.int32, cube, 2), cells_z
    )

    def blocks(matrix):
        wide = jnp.broadcast_to(dot_nn(matrix, spread)[:, None], cube)
        return jnp.where(match, wide, 0.0).reshape(size, size).astype(BF16)

    top, rest = blocks(top), blocks(rest)
    left = jnp.concatenate([top, top, rest], axis=1)
    unscale = scale / jnp.sqrt(weights_ref[...])

    for load in loads:
        load.wait()
    stores = []
    for c in range(3):
        for x in range(0, cells_x, 2):
            a = jnp.concatenate([high[c, x], high[c, x + 1]], axis=1)
            b = jnp.concatenate([low[c, x], low[c, x + 1]], axis=1)
            mixed = dot_nn(left, jnp.concatenate([a, b, a], axis=0))
            for n in range(2):
                cut = mixed[:, n * cells_y : (n + 1) * cells_y]
                out[c, :, x + n] = cut.reshape(snaps, cells_z, cells_y) * unscale[x + n][None]
        copy = pltpu.make_async_copy(out.at[c], out_hbm.at[c], out_sem.at[c])
        copy.start()
        stores.append(copy)
    for copy in stores:
        copy.wait()


def mix_call(scale, shape, gram, weights, high, low):
    dma = pltpu.SemaphoreType.DMA
    return pl.pallas_call(
        functools.partial(mix_kernel, scale),
        out_shape=jax.ShapeDtypeStruct(shape, F32),
        in_specs=[
            pl.BlockSpec(memory_space=pltpu.VMEM),
            pl.BlockSpec(memory_space=pltpu.VMEM),
            pl.BlockSpec(memory_space=pl.ANY),
            pl.BlockSpec(memory_space=pl.ANY),
        ],
        out_specs=pl.BlockSpec(memory_space=pl.ANY),
        scratch_shapes=[
            pltpu.VMEM(high.shape, BF16),
            pltpu.VMEM(low.shape, BF16),
            pltpu.VMEM(shape, F32),
            dma((2, 3)),
            dma((3,)),
        ],
        compiler_params=pltpu.CompilerParams(vmem_limit_bytes=28 << 20),
        name="mix",
    )(gram, weights, high, low)


def solution(mesh):
    placed = (P(None, None, "gx", "gz", None), P("gx", "gz", None))
    axes = (mesh.shape["gx"], mesh.shape["gz"])

    def per_device(velocity, weights):
        rows_all = 3 * weights.size * axes[0] * axes[1]
        scale = float(rows_all) ** 0.5
        gram, high, low = gram_call(axes, velocity, weights)
        return mix_call(scale, velocity.shape, gram, weights, high, low)

    return jax.shard_map(
        per_device,
        mesh=mesh,
        in_specs=placed,
        out_specs=P(None, None, "gx", "gz", None),
        check_vma=False,
    )
```

```python
import functools
import itertools

import jax
import jax.numpy as jnp
from jax import lax
from jax.experimental import pallas as pl
from jax.experimental.pallas import tpu as pltpu
from jax.sharding import PartitionSpec as P

WHOLE = 840.0
COEFS = (672.0, -168.0, 32.0, -3.0)
WIDTH = len(COEFS)
MESH = pl.DeviceIdType.MESH
F32 = jnp.float32
BF16 = jnp.bfloat16
PAIR = 2
U, V, W = 0, 1, 2


def dims_of(count_x, count_z):
    core = 2
    x = 4 if count_x % 8 == 0 else 1
    return {"y": count_x // (core * x), "x": x, "core": core, "z": count_z}


PHASES = (("y", "core"), ("z", "x"))


def offsets_of(names, dims):
    def hops(offset):
        return sum(
            min(d, dims[n] - d) * (0.1 if n == "core" else 1.0)
            for n, d in zip(names, offset, strict=True)
        )

    every = itertools.product(*[range(dims[n]) for n in names])
    return sorted((o for o in every if any(o)), key=lambda o: -hops(o))


def dot_nt(a, b):
    return lax.dot_general(a, b, (((1,), (1,)), ((), ())), preferred_element_type=F32)


def dot_nn(a, b):
    return lax.dot_general(a, b, (((1,), (0,)), ((), ())), preferred_element_type=F32)


def stencil(distance):
    total = jnp.zeros(distance.shape, F32)
    for step, weight in enumerate(COEFS, start=1):
        total = jnp.where(distance == step, weight, total)
        total = jnp.where(distance == -step, -weight, total)
    return total


def iota(shape, dim):
    return lax.broadcasted_iota(jnp.int32, shape, dim)


def gram_kernel(
    axes,
    scale,
    vel_hbm,
    weights_hbm,
    gram_ref,
    high,
    low,
    unscale,
    vel,
    weights,
    halo_x,
    halo_z,
    part,
    span_matrix,
    acc,
    slots,
    vel_sem,
    x_send,
    x_recv,
    z_send,
    z_recv,
    slot_send,
    slot_recv,
):
    snaps, cells_x, cells_z, cells_y = vel_hbm.shape[1:]
    size = snaps * cells_z
    count_x, count_z = axes
    dims = dims_of(count_x, count_z)
    gx, gz = lax.axis_index("gx"), lax.axis_index("gz")
    core_x = dims["x"] * dims["core"]
    mine = {
        "y": gx // core_x,
        "x": lax.rem(gx // dims["core"], dims["x"]),
        "core": lax.rem(gx, dims["core"]),
        "z": gz,
    }

    def peer_at(names, offset):
        place = dict(mine)
        for name, d in zip(names, offset, strict=True):
            if d:
                place[name] = lax.rem(place[name] + d, dims[name])
        return (place["y"] * core_x + place["x"] * dims["core"] + place["core"], place["z"])

    right_x, left_x = lax.rem(gx + 1, count_x), lax.rem(gx + count_x - 1, count_x)
    right_z, left_z = lax.rem(gz + 1, count_z), lax.rem(gz + count_z - 1, count_z)

    barrier = pltpu.get_barrier_semaphore()
    announced = [(right_x, gz), (left_x, gz), (gx, right_z), (gx, left_z)]
    for names in PHASES:
        announced += [peer_at(names, offset) for offset in offsets_of(names, dims)]
    for peer in announced:
        pl.semaphore_signal(barrier, inc=1, device_id=peer, device_id_type=MESH)

    loads = [
        pltpu.make_async_copy(vel_hbm.at[c], vel.at[c], vel_sem.at[c]) for c in (W, U, V)
    ]
    loads.append(pltpu.make_async_copy(weights_hbm, weights, vel_sem.at[3]))
    for load in loads:
        load.start()

    pl.semaphore_wait(barrier, len(announced))

    z_copies = {}
    x_copies = {}

    def start_z(k):
        source = (V, U)[k]
        for first in range(0, cells_x, 2):
            xs = pl.ds(first, 2)
            for side, peer in ((0, (gx, left_z)), (1, (gx, right_z))):
                rows = pl.ds(side * WIDTH, WIDTH)
                copy = pltpu.make_async_remote_copy(
                    src_ref=vel_hbm.at[source, :, xs, rows, :],
                    dst_ref=halo_z.at[k, :, xs, rows, :],
                    send_sem=z_send.at[k, first // 2, side],
                    recv_sem=z_recv.at[k, first // 2, side],
                    device_id=peer,
                    device_id_type=MESH,
                )
                copy.start()
                z_copies[k, first, side] = copy

    def start_x():
        for k, source in enumerate((V, W)):
            for side, peer, first in ((0, (right_x, gz), cells_x - WIDTH), (1, (left_x, gz), 0)):
                copy = pltpu.make_async_remote_copy(
                    src_ref=vel_hbm.at[source, :, pl.ds(first, WIDTH)],
                    dst_ref=halo_x.at[k, side],
                    send_sem=x_send.at[k, side],
                    recv_sem=x_recv.at[k, side],
                    device_id=peer,
                    device_id_type=MESH,
                )
                copy.start()
                x_copies[k, side] = copy

    start_z(0)
    start_x()
    start_z(1)

    wall = stencil(iota((cells_y, cells_y), 0) - iota((cells_y, cells_y), 1)).astype(BF16)
    wide = (size, size)
    to_row, from_row = iota(wide, 0), iota(wide, 1)
    same = to_row // cells_z == from_row // cells_z
    to_z, from_z = lax.rem(to_row, cells_z), lax.rem(from_row, cells_z)
    beyond = jnp.where(from_z < WIDTH, from_z + cells_z, from_z - cells_z)
    for n, source_z in enumerate((from_z, beyond)):
        span_matrix[:, n * size : (n + 1) * size] = jnp.where(
            same, stencil(source_z - to_z), 0.0
        ).astype(BF16)
    acc[...] = jnp.zeros_like(acc)

    for load in loads:
        load.wait()

    root_weights = jnp.sqrt(weights[...])
    root = root_weights * (1.0 / WHOLE)
    unscale[...] = scale / root_weights

    def plane_of(ref, c, x):
        return ref[c, :, x].reshape(size, cells_y)

    @pl.loop(0, cells_x)
    def _(x):
        both = jnp.concatenate([plane_of(vel, W, x), plane_of(vel, U, x)], axis=0)
        part[pl.ds(0, 2), x] = dot_nn(both, wall).reshape(2, size, cells_y)

    def keep(c, x, rows, value):
        scaled = (value.reshape(-1, cells_z, cells_y) * root[x][None]).reshape(value.shape)
        rounded = scaled.astype(BF16)
        high[c, x, rows, :] = rounded
        low[c, x, rows, :] = (scaled - rounded.astype(F32)).astype(BF16)

    def accumulate(c, first, count):
        tops = jnp.concatenate([high[c, first + x] for x in range(count)], axis=1)
        rests = jnp.concatenate([low[c, first + x] for x in range(count)], axis=1)
        acc[...] += dot_nt(jnp.concatenate([tops, rests], axis=0), tops)

    rows_pair = PAIR * cells_z

    def stream(k, i):
        pair = pl.ds(i * PAIR, PAIR)
        ext = jnp.concatenate(
            [
                halo_x[k, 0, pair].astype(F32),
                vel[(V, W)[k], pair].astype(F32),
                halo_x[k, 1, pair].astype(F32),
            ],
            axis=1,
        )
        for x in range(cells_x):
            total = None
            for step, weight in enumerate(COEFS, start=1):
                term = weight * (ext[:, WIDTH + x + step] - ext[:, WIDTH + x - step])
                total = term if total is None else total + term
            yield x, total.reshape(rows_pair, cells_y)

    for side in range(2):
        x_copies[0, side].wait_recv()

    @pl.loop(0, snaps // PAIR)
    def _(i):
        rows = pl.ds(pl.multiple_of(i * rows_pair, rows_pair), rows_pair)
        for x, value in stream(0, i):
            keep(2, x, rows, value - part[1, x, rows])

    for side in range(2):
        x_copies[1, side].wait_recv()

    @pl.loop(0, snaps // PAIR)
    def _(i):
        rows = pl.ds(pl.multiple_of(i * rows_pair, rows_pair), rows_pair)
        for x, value in stream(1, i):
            part[1, x, rows] = value

    for first in range(0, cells_x, 4):
        accumulate(2, first, 4)

    for k, source in enumerate((V, U)):
        for first in range(0, cells_x, 2):
            for side in range(2):
                z_copies[k, first, side].wait_recv()
            xs = (first, first + 1)
            inner = jnp.concatenate([plane_of(vel, source, x) for x in xs], axis=1)
            beside = jnp.concatenate([plane_of(halo_z, k, x) for x in xs], axis=1)
            span = dot_nn(span_matrix[...], jnp.concatenate([inner, beside], axis=0))
            for n, x in enumerate(xs):
                cut = span[:, n * cells_y : (n + 1) * cells_y]
                keep(k, x, slice(None), part[0, x] - cut if k == 0 else cut - part[1, x])
            accumulate(k, first, 2)

    square = acc[...].reshape(2 * snaps, cells_z, size)
    match = iota(square.shape, 1) == lax.rem(iota(square.shape, 2), cells_z)
    matched = jnp.where(match, square, 0.0).sum(axis=1)
    matched = 0.5 * matched[:snaps] + matched[snaps:]
    per_row, lanes = gram_ref.shape
    gather = (iota((size, lanes), 0) // cells_z == iota((size, lanes), 1)).astype(BF16)
    one = matched.astype(BF16)
    rest = matched - one.astype(F32)
    two = rest.astype(BF16)
    three = (rest - two.astype(F32)).astype(BF16)
    half = dot_nn(jnp.concatenate([one, two, three], axis=0), gather)
    half = half[:snaps] + half[snaps : 2 * snaps] + half[2 * snaps :]
    packed = half[:per_row]
    for q in range(1, snaps // per_row):
        packed += pltpu.roll(half[q * per_row : (q + 1) * per_row], q * snaps, 1)

    slot_copies = []
    value = packed
    base = 0
    for phase, names in enumerate(PHASES):
        offsets = offsets_of(names, dims)
        slots[base] = value
        for n, offset in enumerate(offsets, start=1):
            pltpu.make_async_remote_copy(
                src_ref=slots.at[base],
                dst_ref=slots.at[base + n],
                send_sem=slot_send.at[phase],
                recv_sem=slot_recv.at[phase],
                device_id=peer_at(names, offset),
                device_id_type=MESH,
            ).start()
        landed = slots.at[pl.ds(base + 1, len(offsets))]
        everything = pltpu.make_async_remote_copy(
            src_ref=landed,
            dst_ref=landed,
            send_sem=slot_send.at[phase],
            recv_sem=slot_recv.at[phase],
            device_id=peer_at(names, offsets[0]),
            device_id_type=MESH,
        )
        everything.wait_recv()
        slot_copies.append(everything)
        terms = [slots[base + n] for n in range(len(offsets) + 1)]
        while len(terms) > 1:
            terms = [sum(terms[j + 1 : j + 2], terms[j]) for j in range(0, len(terms), 2)]
        value = terms[0]
        base += len(offsets) + 1
    gram_ref[...] = value

    for copy in slot_copies:
        copy.wait_send()
    for copy in x_copies.values():
        copy.wait_send()
    for copy in z_copies.values():
        copy.wait_send()


def gram_call(axes, scale, velocity, weights):
    _, snaps, cells_x, cells_z, cells_y = velocity.shape
    size = snaps * cells_z
    held = jax.ShapeDtypeStruct((3, cells_x, size, cells_y), BF16)
    dma = pltpu.SemaphoreType.DMA
    dims = dims_of(*axes)
    tiles = sum(len(offsets_of(names, dims)) + 1 for names in PHASES)
    return pl.pallas_call(
        functools.partial(gram_kernel, axes, scale),
        out_shape=(
            jax.ShapeDtypeStruct((8, 128), F32),
            held,
            held,
            jax.ShapeDtypeStruct(weights.shape, F32),
        ),
        in_specs=[pl.BlockSpec(memory_space=pltpu.HBM)] * 2,
        out_specs=(pl.BlockSpec(memory_space=pltpu.VMEM),) * 4,
        scratch_shapes=[
            pltpu.VMEM(velocity.shape, BF16),
            pltpu.VMEM(weights.shape, F32),
            pltpu.VMEM((2, 2, snaps, WIDTH, cells_z, cells_y), BF16),
            pltpu.VMEM((2, snaps, cells_x, cells_z, cells_y), BF16),
            pltpu.VMEM((2, cells_x, size, cells_y), F32),
            pltpu.VMEM((size, 2 * size), BF16),
            pltpu.VMEM((2 * size, size), F32),
            pltpu.VMEM((tiles, 8, 128), F32),
            dma((4,)),
            dma((2, 2)),
            dma((2, 2)),
            dma((2, cells_x // 2, 2)),
            dma((2, cells_x // 2, 2)),
            dma((len(PHASES),)),
            dma((len(PHASES),)),
        ],
        compiler_params=pltpu.CompilerParams(
            collective_id=0, has_side_effects=True, vmem_limit_bytes=28 << 20
        ),
        name="curl_gram",
    )(velocity, weights)


BLOCK = 8


def eliminate(gram):
    snaps, lanes = gram.shape
    tile = 8
    lane = iota((tile, lanes), 1)
    row = iota((tile, lanes), 0)
    full = (tile, lanes)
    work = []
    for t in range(snaps // tile):
        unit = jnp.where(lane == row + snaps + t * tile, 1.0, 0.0)
        work.append(jnp.where(lane < snaps, gram[t * tile : (t + 1) * tile], unit))
    roots = [jnp.ones(full, F32) for _ in work]
    for b in range(0, snaps, BLOCK):
        steps = range(BLOCK)
        home, at = b // tile, [(b + j) % tile for j in steps]
        rows = [jnp.broadcast_to(work[home][at[j] : at[j] + 1], full) for j in steps]
        columns = [
            {
                t: jnp.broadcast_to(work[t][:, b + j : b + j + 1], full)
                for t in range(home, len(work))
            }
            for j in steps
        ]
        cross = [
            [jnp.broadcast_to(columns[j][home][at[i] : at[i] + 1], full) for j in steps]
            for i in steps
        ]
        for j in steps:
            pivot = cross[j][j]
            inverse = 1.0 / pivot
            roots[home] = jnp.where(row == at[j], pivot, roots[home])
            factors = {t: columns[j][t] * inverse for t in columns[j]}
            factors[home] = jnp.where(row > at[j], factors[home], 0.0)
            for m in steps[j + 1 :]:
                for t in columns[m]:
                    columns[m][t] = columns[m][t] - factors[t] * cross[j][m]
            for i in steps[j + 1 :]:
                ratio = cross[i][j] * inverse
                rows[i] = rows[i] - ratio * rows[j]
                for m in steps[j + 1 :]:
                    cross[i][m] = cross[i][m] - ratio * cross[j][m]
            for t in columns[j]:
                work[t] = work[t] - factors[t] * rows[j]
    return jnp.concatenate([w / jnp.sqrt(r) for w, r in zip(work, roots, strict=True)], axis=0)


def mix_kernel(gram_ref, unscale, high, low, out_hbm, out, out_sem):
    _, cells_x, size, cells_y = high.shape
    snaps = out.shape[1]
    cells_z = size // snaps

    packed = gram_ref[...]
    lanes = packed.shape[1]
    pieces = [packed] + [
        pltpu.roll(packed, lanes - q * snaps, 1) for q in range(1, lanes // snaps)
    ]
    half = jnp.concatenate(pieces, axis=0)
    half = jnp.where(iota(half.shape, 1) < snaps, half, 0.0)
    tall = jnp.concatenate([half, jnp.zeros((lanes - snaps, lanes), F32)], axis=0)
    inverse = eliminate(half + tall.T[:snaps])
    place = iota(inverse.shape, 1)
    inverse = jnp.where((place >= snaps) & (place < 2 * snaps), inverse, 0.0)

    spread = (iota((lanes, size), 0) == snaps + iota((lanes, size), 1) // cells_z).astype(BF16)
    top = inverse.astype(BF16)
    rest = (inverse - top.astype(F32)).astype(BF16)
    spans = dot_nn(jnp.concatenate([top, rest], axis=0), spread)
    cube = (2 * snaps, cells_z, size)
    match = iota(cube, 1) == lax.rem(iota(cube, 2), cells_z)
    left = jnp.where(match, jnp.broadcast_to(spans[:, None], cube), 0.0)
    left = left.reshape(2 * size, size).astype(BF16)

    stores = []
    for c in range(3):
        for first in range(0, cells_x, 2):
            xs = (first, first + 1)
            a = jnp.concatenate([high[c, x] for x in xs], axis=1)
            b = jnp.concatenate([low[c, x] for x in xs], axis=1)
            mixed = dot_nn(left, a)
            mixed = mixed[:size] + mixed[size:] + dot_nn(left[:size], b)
            for n, x in enumerate(xs):
                cut = mixed[:, n * cells_y : (n + 1) * cells_y]
                out[c, :, x] = cut.reshape(snaps, cells_z, cells_y) * unscale[x][None]
            where = (c, slice(None), pl.ds(first, 2))
            copy = pltpu.make_async_copy(
                out.at[where], out_hbm.at[where], out_sem.at[c, first // 2]
            )
            copy.start()
            stores.append(copy)
    for copy in stores:
        copy.wait()


def mix_call(shape, gram, unscale, high, low):
    return pl.pallas_call(
        mix_kernel,
        out_shape=jax.ShapeDtypeStruct(shape, F32),
        in_specs=[pl.BlockSpec(memory_space=pltpu.VMEM)] * 4,
        out_specs=pl.BlockSpec(memory_space=pltpu.HBM),
        scratch_shapes=[
            pltpu.VMEM(shape, F32),
            pltpu.SemaphoreType.DMA((3, shape[2] // 2)),
        ],
        compiler_params=pltpu.CompilerParams(vmem_limit_bytes=28 << 20),
        name="mix",
    )(gram, unscale, high, low)


def solution(mesh):
    placed = (P(None, None, "gx", "gz", None), P("gx", "gz", None))
    axes = (mesh.shape["gx"], mesh.shape["gz"])

    def per_device(velocity, weights):
        rows_all = 3 * weights.size * axes[0] * axes[1]
        scale = float(rows_all) ** 0.5
        velocity, weights = (
            pltpu.with_memory_space_constraint(a, pltpu.HBM) for a in (velocity, weights)
        )
        gram, high, low, unscale = gram_call(axes, scale, velocity, weights)
        return mix_call(velocity.shape, gram, unscale, high, low)

    return jax.shard_map(
        per_device,
        mesh=mesh,
        in_specs=placed,
        out_specs=P(None, None, "gx", "gz", None),
        check_vma=False,
    )
```

```python
import functools
import itertools

import jax
import jax.numpy as jnp
from jax import lax
from jax.experimental import pallas as pl
from jax.experimental.pallas import tpu as pltpu
from jax.sharding import PartitionSpec as P

WHOLE = 840.0
COEFS = (672.0, -168.0, 32.0, -3.0)
WIDTH = len(COEFS)
MESH = pl.DeviceIdType.MESH
F32 = jnp.float32
BF16 = jnp.bfloat16
PAIR = 2
U, V, W = 0, 1, 2


def dims_of(count_x, count_z):
    core = 2
    x = 4 if count_x % 8 == 0 else 1
    return {"y": count_x // (core * x), "x": x, "core": core, "z": count_z}


PHASES = (("y", "core"), ("z", "x"))
ROUNDS = 8


def offsets_of(names, dims):
    def hops(offset):
        return sum(
            min(d, dims[n] - d) * (0.1 if n == "core" else 1.0)
            for n, d in zip(names, offset, strict=True)
        )

    every = itertools.product(*[range(dims[n]) for n in names])
    return sorted((o for o in every if any(o)), key=lambda o: -hops(o))


def dot_nt(a, b):
    return lax.dot_general(a, b, (((1,), (1,)), ((), ())), preferred_element_type=F32)


def dot_nn(a, b):
    return lax.dot_general(a, b, (((1,), (0,)), ((), ())), preferred_element_type=F32)


def stencil(distance):
    total = jnp.zeros(distance.shape, F32)
    for step, weight in enumerate(COEFS, start=1):
        total = jnp.where(distance == step, weight, total)
        total = jnp.where(distance == -step, -weight, total)
    return total


def iota(shape, dim):
    return lax.broadcasted_iota(jnp.int32, shape, dim)


def gram_kernel(
    axes,
    scale,
    vel_hbm,
    weights_hbm,
    gram_ref,
    high,
    low,
    unscale,
    vel,
    weights,
    halo_x,
    halo_z,
    part,
    span_matrix,
    acc,
    slots,
    vel_sem,
    x_send,
    x_recv,
    z_send,
    z_recv,
    slot_send,
    slot_recv,
    news,
):
    snaps, cells_x, cells_z, cells_y = vel_hbm.shape[1:]
    size = snaps * cells_z
    count_x, count_z = axes
    dims = dims_of(count_x, count_z)
    gx, gz = lax.axis_index("gx"), lax.axis_index("gz")
    core_x = dims["x"] * dims["core"]
    mine = {
        "y": gx // core_x,
        "x": lax.rem(gx // dims["core"], dims["x"]),
        "core": lax.rem(gx, dims["core"]),
        "z": gz,
    }

    def peer_at(names, offset):
        place = dict(mine)
        for name, d in zip(names, offset, strict=True):
            if d:
                place[name] = lax.rem(place[name] + d, dims[name])
        return (place["y"] * core_x + place["x"] * dims["core"] + place["core"], place["z"])

    right_x, left_x = lax.rem(gx + 1, count_x), lax.rem(gx + count_x - 1, count_x)
    right_z, left_z = lax.rem(gz + 1, count_z), lax.rem(gz + count_z - 1, count_z)

    def beside(*names):
        return [
            peer_at((name,), (step,)) for name in names for step in (1, dims[name] - 1) if step
        ]

    def signal(semaphore, peers):
        for peer in peers:
            pl.semaphore_signal(semaphore, inc=1, device_id=peer, device_id_type=MESH)

    barrier = pltpu.get_barrier_semaphore()
    direct = [(right_x, gz), (left_x, gz)] + beside("z", "y", "x")
    signal(barrier, direct)
    rounds = [beside("x")] * max(dims["x"] // 2 - 1, 0)
    rounds += [beside("z", "y")] * max(dims["z"] // 2, dims["y"] // 2)
    heard = [0]

    def tell():
        if heard[0] < len(rounds):
            signal(news.at[heard[0]], rounds[heard[0]])

    def hear():
        if heard[0] < len(rounds):
            pl.semaphore_wait(news.at[heard[0]], len(rounds[heard[0]]))
            heard[0] += 1
            tell()

    loads = [
        pltpu.make_async_copy(vel_hbm.at[c], vel.at[c], vel_sem.at[c]) for c in (W, U, V)
    ]
    loads.append(pltpu.make_async_copy(weights_hbm, weights, vel_sem.at[3]))
    for load in loads:
        load.start()

    pl.semaphore_wait(barrier, len(direct))

    z_copies = {}
    x_copies = {}

    def start_z(k):
        source = (V, U)[k]
        for first in range(0, cells_x, 2):
            xs = pl.ds(first, 2)
            for side, peer in ((0, (gx, left_z)), (1, (gx, right_z))):
                rows = pl.ds(side * WIDTH, WIDTH)
                copy = pltpu.make_async_remote_copy(
                    src_ref=vel_hbm.at[source, :, xs, rows, :],
                    dst_ref=halo_z.at[k, :, xs, rows, :],
                    send_sem=z_send.at[k, first // 2, side],
                    recv_sem=z_recv.at[k, first // 2, side],
                    device_id=peer,
                    device_id_type=MESH,
                )
                copy.start()
                z_copies[k, first, side] = copy

    def start_x():
        for k, source in enumerate((V, W)):
            for side, peer, first in ((0, (right_x, gz), cells_x - WIDTH), (1, (left_x, gz), 0)):
                copy = pltpu.make_async_remote_copy(
                    src_ref=vel_hbm.at[source, :, pl.ds(first, WIDTH)],
                    dst_ref=halo_x.at[k, side],
                    send_sem=x_send.at[k, side],
                    recv_sem=x_recv.at[k, side],
                    device_id=peer,
                    device_id_type=MESH,
                )
                copy.start()
                x_copies[k, side] = copy

    start_z(0)
    start_x()
    start_z(1)
    tell()

    wall = stencil(iota((cells_y, cells_y), 0) - iota((cells_y, cells_y), 1)).astype(BF16)
    wide = (size, size)
    to_row, from_row = iota(wide, 0), iota(wide, 1)
    to_z, from_z = to_row & (cells_z - 1), from_row & (cells_z - 1)
    same = to_row - to_z == from_row - from_z
    beyond = jnp.where(from_z < WIDTH, from_z + cells_z, from_z - cells_z)
    for n, source_z in enumerate((from_z, beyond)):
        span_matrix[:, n * size : (n + 1) * size] = jnp.where(
            same, stencil(source_z - to_z), 0.0
        ).astype(BF16)

    hear()
    for load in loads:
        load.wait()

    root_weights = jnp.sqrt(weights[...])
    root = root_weights * (1.0 / WHOLE)
    unscale[...] = scale / root_weights

    def plane_of(ref, c, x):
        return ref[c, :, x].reshape(size, cells_y)

    @pl.loop(0, cells_x)
    def _(x):
        both = jnp.concatenate([plane_of(vel, W, x), plane_of(vel, U, x)], axis=0)
        part[pl.ds(0, 2), x] = dot_nn(both, wall).reshape(2, size, cells_y)

    def keep(c, x, rows, value):
        scaled = (value.reshape(-1, cells_z, cells_y) * root[x][None]).reshape(value.shape)
        rounded = scaled.astype(BF16)
        high[c, x, rows, :] = rounded
        low[c, x, rows, :] = (scaled - rounded.astype(F32)).astype(BF16)

    def product(c, first, count):
        tops = jnp.concatenate([high[c, first + x] for x in range(count)], axis=1)
        rests = jnp.concatenate([low[c, first + x] for x in range(count)], axis=1)
        return dot_nt(jnp.concatenate([tops, rests], axis=0), tops)

    rows_pair = PAIR * cells_z

    def stream(k, i):
        pair = pl.ds(i * PAIR, PAIR)
        ext = jnp.concatenate(
            [
                halo_x[k, 0, pair].astype(F32),
                vel[(V, W)[k], pair].astype(F32),
                halo_x[k, 1, pair].astype(F32),
            ],
            axis=1,
        )
        for x in range(cells_x):
            total = None
            for step, weight in enumerate(COEFS, start=1):
                term = weight * (ext[:, WIDTH + x + step] - ext[:, WIDTH + x - step])
                total = term if total is None else total + term
            yield x, total.reshape(rows_pair, cells_y)

    hear()
    for side in range(2):
        x_copies[0, side].wait_recv()

    @pl.loop(0, snaps // PAIR)
    def _(i):
        rows = pl.ds(pl.multiple_of(i * rows_pair, rows_pair), rows_pair)
        for x, value in stream(0, i):
            keep(2, x, rows, value - part[1, x, rows])

    hear()
    for side in range(2):
        x_copies[1, side].wait_recv()

    @pl.loop(0, snaps // PAIR)
    def _(i):
        rows = pl.ds(pl.multiple_of(i * rows_pair, rows_pair), rows_pair)
        for x, value in stream(1, i):
            part[1, x, rows] = value

    hear()
    acc[...] = product(2, 0, cells_x // 2)
    acc[...] += product(2, cells_x // 2, cells_x // 2)

    for k, source in enumerate((V, U)):
        for first in range(0, cells_x, 2):
            for side in range(2):
                z_copies[k, first, side].wait_recv()
            xs = (first, first + 1)
            inner = jnp.concatenate([plane_of(vel, source, x) for x in xs], axis=1)
            outer = jnp.concatenate([plane_of(halo_z, k, x) for x in xs], axis=1)
            span = dot_nn(span_matrix[...], jnp.concatenate([inner, outer], axis=0))
            for n, x in enumerate(xs):
                cut = span[:, n * cells_y : (n + 1) * cells_y]
                keep(k, x, slice(None), part[0, x] - cut if k == 0 else cut - part[1, x])
            if k == 0 or first + 2 < cells_x:
                acc[...] += product(k, first, 2)
        if k == 0:
            for _ in range(len(rounds)):
                hear()

    square = (acc[...] + product(1, cells_x - 2, 2)).reshape(2 * snaps, cells_z, size)
    match = iota((cells_z, size), 0) == iota((cells_z, size), 1) & (cells_z - 1)
    matched = jnp.where(match[None], square, 0.0).sum(axis=1)
    matched = 0.5 * matched[:snaps] + matched[snaps:]
    per_row, lanes = gram_ref.shape
    ahead = iota((size, lanes), 0) - cells_z * iota((size, lanes), 1)
    gather = ((ahead >= 0) & (ahead < cells_z)).astype(BF16)
    one = matched.astype(BF16)
    rest = matched - one.astype(F32)
    two = rest.astype(BF16)
    three = (rest - two.astype(F32)).astype(BF16)
    half = dot_nn(jnp.concatenate([one, two, three], axis=0), gather)
    half = half[:snaps] + half[snaps : 2 * snaps] + half[2 * snaps :]
    packed = half[:per_row]
    for q in range(1, snaps // per_row):
        packed += pltpu.roll(half[q * per_row : (q + 1) * per_row], q * snaps, 1)

    slot_copies = []
    value = packed
    base = 0
    for phase, names in enumerate(PHASES):
        offsets = offsets_of(names, dims)
        slots[base] = value
        for n, offset in enumerate(offsets, start=1):
            pltpu.make_async_remote_copy(
                src_ref=slots.at[base],
                dst_ref=slots.at[base + n],
                send_sem=slot_send.at[phase],
                recv_sem=slot_recv.at[phase],
                device_id=peer_at(names, offset),
                device_id_type=MESH,
            ).start()
        landed = slots.at[pl.ds(base + 1, len(offsets))]
        everything = pltpu.make_async_remote_copy(
            src_ref=landed,
            dst_ref=landed,
            send_sem=slot_send.at[phase],
            recv_sem=slot_recv.at[phase],
            device_id=peer_at(names, offsets[0]),
            device_id_type=MESH,
        )
        everything.wait_recv()
        slot_copies.append(everything)
        terms = [slots[base + n] for n in range(len(offsets) + 1)]
        while len(terms) > 1:
            terms = [sum(terms[j + 1 : j + 2], terms[j]) for j in range(0, len(terms), 2)]
        value = terms[0]
        base += len(offsets) + 1
    gram_ref[...] = value

    for copy in slot_copies:
        copy.wait_send()
    for copy in x_copies.values():
        copy.wait_send()
    for copy in z_copies.values():
        copy.wait_send()


def gram_call(axes, scale, velocity, weights):
    _, snaps, cells_x, cells_z, cells_y = velocity.shape
    size = snaps * cells_z
    held = jax.ShapeDtypeStruct((3, cells_x, size, cells_y), BF16)
    dma = pltpu.SemaphoreType.DMA
    dims = dims_of(*axes)
    tiles = sum(len(offsets_of(names, dims)) + 1 for names in PHASES)
    return pl.pallas_call(
        functools.partial(gram_kernel, axes, scale),
        out_shape=(
            jax.ShapeDtypeStruct((8, 128), F32),
            held,
            held,
            jax.ShapeDtypeStruct(weights.shape, F32),
        ),
        in_specs=[pl.BlockSpec(memory_space=pltpu.HBM)] * 2,
        out_specs=(pl.BlockSpec(memory_space=pltpu.VMEM),) * 4,
        scratch_shapes=[
            pltpu.VMEM(velocity.shape, BF16),
            pltpu.VMEM(weights.shape, F32),
            pltpu.VMEM((2, 2, snaps, WIDTH, cells_z, cells_y), BF16),
            pltpu.VMEM((2, snaps, cells_x, cells_z, cells_y), BF16),
            pltpu.VMEM((2, cells_x, size, cells_y), F32),
            pltpu.VMEM((size, 2 * size), BF16),
            pltpu.VMEM((2 * size, size), F32),
            pltpu.VMEM((tiles, 8, 128), F32),
            dma((4,)),
            dma((2, 2)),
            dma((2, 2)),
            dma((2, cells_x // 2, 2)),
            dma((2, cells_x // 2, 2)),
            dma((len(PHASES),)),
            dma((len(PHASES),)),
            pltpu.SemaphoreType.REGULAR((ROUNDS,)),
        ],
        compiler_params=pltpu.CompilerParams(
            collective_id=0, has_side_effects=True, vmem_limit_bytes=28 << 20
        ),
        name="curl_gram",
    )(velocity, weights)


BLOCK = 8


def eliminate(gram):
    snaps, lanes = gram.shape
    tile = 8
    lane = iota((tile, lanes), 1)
    row = iota((tile, lanes), 0)
    full = (tile, lanes)
    work = []
    for t in range(snaps // tile):
        unit = jnp.where(lane == row + snaps + t * tile, 1.0, 0.0)
        work.append(jnp.where(lane < snaps, gram[t * tile : (t + 1) * tile], unit))
    roots = [jnp.ones(full, F32) for _ in work]
    for b in range(0, snaps, BLOCK):
        steps = range(BLOCK)
        home, at = b // tile, [(b + j) % tile for j in steps]
        rows = [jnp.broadcast_to(work[home][at[j] : at[j] + 1], full) for j in steps]
        columns = [
            {
                t: jnp.broadcast_to(work[t][:, b + j : b + j + 1], full)
                for t in range(home, len(work))
            }
            for j in steps
        ]
        cross = [
            [jnp.broadcast_to(columns[j][home][at[i] : at[i] + 1], full) for j in steps]
            for i in steps
        ]
        for j in steps:
            pivot = cross[j][j]
            inverse = 1.0 / pivot
            roots[home] = jnp.where(row == at[j], pivot, roots[home])
            factors = {t: columns[j][t] * inverse for t in columns[j]}
            factors[home] = jnp.where(row > at[j], factors[home], 0.0)
            for m in steps[j + 1 :]:
                for t in columns[m]:
                    columns[m][t] = columns[m][t] - factors[t] * cross[j][m]
            for i in steps[j + 1 :]:
                ratio = cross[i][j] * inverse
                rows[i] = rows[i] - ratio * rows[j]
                for m in steps[j + 1 :]:
                    cross[i][m] = cross[i][m] - ratio * cross[j][m]
            for t in columns[j]:
                work[t] = work[t] - factors[t] * rows[j]
    return jnp.concatenate([w / jnp.sqrt(r) for w, r in zip(work, roots, strict=True)], axis=0)


def mix_kernel(gram_ref, unscale, high, low, out_hbm, out, out_sem):
    _, cells_x, size, cells_y = high.shape
    snaps = out.shape[1]
    cells_z = size // snaps

    packed = gram_ref[...]
    lanes = packed.shape[1]
    pieces = [packed] + [
        pltpu.roll(packed, lanes - q * snaps, 1) for q in range(1, lanes // snaps)
    ]
    half = jnp.concatenate(pieces, axis=0)
    half = jnp.where(iota(half.shape, 1) < snaps, half, 0.0)
    tall = jnp.concatenate([half, jnp.zeros((lanes - snaps, lanes), F32)], axis=0)
    inverse = eliminate(half + tall.T[:snaps])
    place = iota(inverse.shape, 1)
    inverse = jnp.where((place >= snaps) & (place < 2 * snaps), inverse, 0.0)

    ahead = iota((lanes, size), 1) - cells_z * (iota((lanes, size), 0) - snaps)
    spread = ((ahead >= 0) & (ahead < cells_z)).astype(BF16)
    top = inverse.astype(BF16)
    rest = (inverse - top.astype(F32)).astype(BF16)
    spans = dot_nn(jnp.concatenate([top, rest], axis=0), spread)
    match = iota((cells_z, size), 0) == iota((cells_z, size), 1) & (cells_z - 1)
    left = jnp.where(match[None], jnp.broadcast_to(spans[:, None], (2 * snaps, cells_z, size)), 0.0)
    left = left.reshape(2 * size, size).astype(BF16)

    stores = []
    for c in range(3):
        for first in range(0, cells_x, 2):
            xs = (first, first + 1)
            a = jnp.concatenate([high[c, x] for x in xs], axis=1)
            b = jnp.concatenate([low[c, x] for x in xs], axis=1)
            mixed = dot_nn(left, a)
            mixed = mixed[:size] + mixed[size:] + dot_nn(left[:size], b)
            for n, x in enumerate(xs):
                cut = mixed[:, n * cells_y : (n + 1) * cells_y]
                out[c, :, x] = cut.reshape(snaps, cells_z, cells_y) * unscale[x][None]
            where = (c, slice(None), pl.ds(first, 2))
            copy = pltpu.make_async_copy(
                out.at[where], out_hbm.at[where], out_sem.at[c, first // 2]
            )
            copy.start()
            stores.append(copy)
    for copy in stores:
        copy.wait()


def mix_call(shape, gram, unscale, high, low):
    return pl.pallas_call(
        mix_kernel,
        out_shape=jax.ShapeDtypeStruct(shape, F32),
        in_specs=[pl.BlockSpec(memory_space=pltpu.VMEM)] * 4,
        out_specs=pl.BlockSpec(memory_space=pltpu.HBM),
        scratch_shapes=[
            pltpu.VMEM(shape, F32),
            pltpu.SemaphoreType.DMA((3, shape[2] // 2)),
        ],
        compiler_params=pltpu.CompilerParams(vmem_limit_bytes=28 << 20),
        name="mix",
    )(gram, unscale, high, low)


def solution(mesh):
    placed = (P(None, None, "gx", "gz", None), P("gx", "gz", None))
    axes = (mesh.shape["gx"], mesh.shape["gz"])

    def per_device(velocity, weights):
        rows_all = 3 * weights.size * axes[0] * axes[1]
        scale = float(rows_all) ** 0.5
        velocity, weights = (
            pltpu.with_memory_space_constraint(a, pltpu.HBM) for a in (velocity, weights)
        )
        gram, high, low, unscale = gram_call(axes, scale, velocity, weights)
        return mix_call(velocity.shape, gram, unscale, high, low)

    return jax.shard_map(
        per_device,
        mesh=mesh,
        in_specs=placed,
        out_specs=P(None, None, "gx", "gz", None),
        check_vma=False,
    )
```

```python
import functools
import itertools

import jax
import jax.numpy as jnp
from jax import lax
from jax.experimental import pallas as pl
from jax.experimental.pallas import tpu as pltpu
from jax.sharding import PartitionSpec as P

WHOLE = 840.0
COEFS = (672.0, -168.0, 32.0, -3.0)
WIDTH = len(COEFS)
MESH = pl.DeviceIdType.MESH
F32 = jnp.float32
BF16 = jnp.bfloat16
PAIR = 2
U, V, W = 0, 1, 2


def dims_of(count_x, count_z):
    core = 2
    x = 4 if count_x % 8 == 0 else 1
    return {"y": count_x // (core * x), "x": x, "core": core, "z": count_z}


PHASES = (("y", "core"), ("z", "x"))
ROUNDS = 8


def offsets_of(names, dims):
    def hops(offset):
        return sum(
            min(d, dims[n] - d) * (0.1 if n == "core" else 1.0)
            for n, d in zip(names, offset, strict=True)
        )

    every = itertools.product(*[range(dims[n]) for n in names])
    return sorted((o for o in every if any(o)), key=lambda o: -hops(o))


def dot_nt(a, b):
    return lax.dot_general(a, b, (((1,), (1,)), ((), ())), preferred_element_type=F32)


def dot_nn(a, b):
    return lax.dot_general(a, b, (((1,), (0,)), ((), ())), preferred_element_type=F32)


def stencil(distance):
    total = jnp.zeros(distance.shape, F32)
    for step, weight in enumerate(COEFS, start=1):
        total = jnp.where(distance == step, weight, total)
        total = jnp.where(distance == -step, -weight, total)
    return total


def iota(shape, dim):
    return lax.broadcasted_iota(jnp.int32, shape, dim)


def gram_kernel(
    axes,
    scale,
    vel_hbm,
    weights_hbm,
    gram_ref,
    high,
    low,
    unscale,
    vel,
    weights,
    halo_x,
    halo_z,
    part,
    span_matrix,
    acc,
    slots,
    vel_sem,
    x_send,
    x_recv,
    z_send,
    z_recv,
    slot_send,
    slot_recv,
    news,
):
    snaps, cells_x, cells_z, cells_y = vel_hbm.shape[1:]
    size = snaps * cells_z
    count_x, count_z = axes
    dims = dims_of(count_x, count_z)
    gx, gz = lax.axis_index("gx"), lax.axis_index("gz")
    core_x = dims["x"] * dims["core"]
    mine = {
        "y": gx // core_x,
        "x": lax.rem(gx // dims["core"], dims["x"]),
        "core": lax.rem(gx, dims["core"]),
        "z": gz,
    }

    def peer_at(names, offset):
        place = dict(mine)
        for name, d in zip(names, offset, strict=True):
            if d:
                place[name] = lax.rem(place[name] + d, dims[name])
        return (place["y"] * core_x + place["x"] * dims["core"] + place["core"], place["z"])

    right_x, left_x = lax.rem(gx + 1, count_x), lax.rem(gx + count_x - 1, count_x)
    right_z, left_z = lax.rem(gz + 1, count_z), lax.rem(gz + count_z - 1, count_z)

    def beside(*names):
        return [
            peer_at((name,), (step,)) for name in names for step in (1, dims[name] - 1) if step
        ]

    def signal(semaphore, peers):
        for peer in peers:
            pl.semaphore_signal(semaphore, inc=1, device_id=peer, device_id_type=MESH)

    barrier = pltpu.get_barrier_semaphore()
    direct = [(right_x, gz), (left_x, gz)] + beside("z", "y", "x")
    signal(barrier, direct)
    rounds = [beside("x")] * max(dims["x"] // 2 - 1, 0)
    rounds += [beside("z", "y")] * max(dims["z"] // 2, dims["y"] // 2)
    heard = [0]

    def tell():
        if heard[0] < len(rounds):
            signal(news.at[heard[0]], rounds[heard[0]])

    def hear():
        if heard[0] < len(rounds):
            pl.semaphore_wait(news.at[heard[0]], len(rounds[heard[0]]))
            heard[0] += 1
            tell()

    loads = [
        pltpu.make_async_copy(vel_hbm.at[c], vel.at[c], vel_sem.at[c]) for c in (W, U, V)
    ]
    loads.append(pltpu.make_async_copy(weights_hbm, weights, vel_sem.at[3]))
    for load in loads:
        load.start()

    pl.semaphore_wait(barrier, len(direct))

    z_copies = {}
    x_copies = {}

    def start_z(k):
        source = (V, U)[k]
        for first in range(0, cells_x, 2):
            xs = pl.ds(first, 2)
            for side, peer in ((0, (gx, left_z)), (1, (gx, right_z))):
                rows = pl.ds(side * WIDTH, WIDTH)
                copy = pltpu.make_async_remote_copy(
                    src_ref=vel_hbm.at[source, :, xs, rows, :],
                    dst_ref=halo_z.at[k, :, xs, rows, :],
                    send_sem=z_send.at[k, first // 2, side],
                    recv_sem=z_recv.at[k, first // 2, side],
                    device_id=peer,
                    device_id_type=MESH,
                )
                copy.start()
                z_copies[k, first, side] = copy

    def start_x():
        for k, source in enumerate((V, W)):
            for side, peer, first in ((0, (right_x, gz), cells_x - WIDTH), (1, (left_x, gz), 0)):
                copy = pltpu.make_async_remote_copy(
                    src_ref=vel_hbm.at[source, :, pl.ds(first, WIDTH)],
                    dst_ref=halo_x.at[k, side],
                    send_sem=x_send.at[k, side],
                    recv_sem=x_recv.at[k, side],
                    device_id=peer,
                    device_id_type=MESH,
                )
                copy.start()
                x_copies[k, side] = copy

    start_z(0)
    start_x()
    start_z(1)
    tell()

    wall = stencil(iota((cells_y, cells_y), 0) - iota((cells_y, cells_y), 1)).astype(BF16)
    wide = (size, size)
    to_row, from_row = iota(wide, 0), iota(wide, 1)
    to_z, from_z = to_row & (cells_z - 1), from_row & (cells_z - 1)
    same = to_row - to_z == from_row - from_z
    beyond = jnp.where(from_z < WIDTH, from_z + cells_z, from_z - cells_z)
    for n, source_z in enumerate((from_z, beyond)):
        span_matrix[:, n * size : (n + 1) * size] = jnp.where(
            same, stencil(source_z - to_z), 0.0
        ).astype(BF16)

    hear()
    for load in loads:
        load.wait()

    root_weights = jnp.sqrt(weights[...])
    root = root_weights * (1.0 / WHOLE)
    unscale[...] = scale / root_weights

    def plane_of(ref, c, x):
        return ref[c, :, x].reshape(size, cells_y)

    @pl.loop(0, cells_x)
    def _(x):
        both = jnp.concatenate([plane_of(vel, W, x), plane_of(vel, U, x)], axis=0)
        part[pl.ds(0, 2), x] = dot_nn(both, wall).reshape(2, size, cells_y)

    def keep(c, x, rows, value):
        scaled = (value.reshape(-1, cells_z, cells_y) * root[x][None]).reshape(value.shape)
        rounded = scaled.astype(BF16)
        high[c, x, rows, :] = rounded
        low[c, x, rows, :] = (scaled - rounded.astype(F32)).astype(BF16)

    def product(c, first, count):
        tops = jnp.concatenate([high[c, first + x] for x in range(count)], axis=1)
        rests = jnp.concatenate([low[c, first + x] for x in range(count)], axis=1)
        return dot_nt(jnp.concatenate([tops, rests], axis=0), tops)

    rows_pair = PAIR * cells_z

    def stream(k, i):
        pair = pl.ds(i * PAIR, PAIR)
        ext = jnp.concatenate(
            [
                halo_x[k, 0, pair].astype(F32),
                vel[(V, W)[k], pair].astype(F32),
                halo_x[k, 1, pair].astype(F32),
            ],
            axis=1,
        )
        for x in range(cells_x):
            total = None
            for step, weight in enumerate(COEFS, start=1):
                term = weight * (ext[:, WIDTH + x + step] - ext[:, WIDTH + x - step])
                total = term if total is None else total + term
            yield x, total.reshape(rows_pair, cells_y)

    hear()
    for side in range(2):
        x_copies[0, side].wait_recv()

    @pl.loop(0, snaps // PAIR)
    def _(i):
        rows = pl.ds(pl.multiple_of(i * rows_pair, rows_pair), rows_pair)
        for x, value in stream(0, i):
            keep(2, x, rows, value - part[1, x, rows])

    hear()
    for side in range(2):
        x_copies[1, side].wait_recv()

    @pl.loop(0, snaps // PAIR)
    def _(i):
        rows = pl.ds(pl.multiple_of(i * rows_pair, rows_pair), rows_pair)
        for x, value in stream(1, i):
            part[1, x, rows] = value

    hear()
    acc[...] = product(2, 0, cells_x // 2)
    acc[...] += product(2, cells_x // 2, cells_x // 2)

    for k, source in enumerate((V, U)):
        for first in range(0, cells_x, 2):
            for side in range(2):
                z_copies[k, first, side].wait_recv()
            xs = (first, first + 1)
            inner = jnp.concatenate([plane_of(vel, source, x) for x in xs], axis=1)
            outer = jnp.concatenate([plane_of(halo_z, k, x) for x in xs], axis=1)
            span = dot_nn(span_matrix[...], jnp.concatenate([inner, outer], axis=0))
            for n, x in enumerate(xs):
                cut = span[:, n * cells_y : (n + 1) * cells_y]
                keep(k, x, slice(None), part[0, x] - cut if k == 0 else cut - part[1, x])
            if k == 0 or first + 2 < cells_x:
                acc[...] += product(k, first, 2)
        if k == 0:
            for _ in range(len(rounds)):
                hear()

    square = acc[...] + product(1, cells_x - 2, 2)
    square = (0.5 * square[:size] + square[size:]).reshape(snaps, cells_z, size)
    match = iota((cells_z, size), 0) == iota((cells_z, size), 1) & (cells_z - 1)
    matched = jnp.where(match[None], square, 0.0).sum(axis=1)
    per_row, lanes = gram_ref.shape
    ahead = iota((size, lanes), 0) - cells_z * iota((size, lanes), 1)
    gather = ((ahead >= 0) & (ahead < cells_z)).astype(BF16)
    one = matched.astype(BF16)
    rest = matched - one.astype(F32)
    two = rest.astype(BF16)
    three = (rest - two.astype(F32)).astype(BF16)
    half = dot_nn(jnp.concatenate([one, two, three], axis=0), gather)
    half = half[:snaps] + half[snaps : 2 * snaps] + half[2 * snaps :]
    packed = half[:per_row]
    for q in range(1, snaps // per_row):
        packed += pltpu.roll(half[q * per_row : (q + 1) * per_row], q * snaps, 1)

    slot_copies = []
    value = packed
    base = 0
    for phase, names in enumerate(PHASES):
        offsets = offsets_of(names, dims)
        slots[base] = value
        for n, offset in enumerate(offsets, start=1):
            pltpu.make_async_remote_copy(
                src_ref=slots.at[base],
                dst_ref=slots.at[base + n],
                send_sem=slot_send.at[phase],
                recv_sem=slot_recv.at[phase],
                device_id=peer_at(names, offset),
                device_id_type=MESH,
            ).start()
        landed = slots.at[pl.ds(base + 1, len(offsets))]
        everything = pltpu.make_async_remote_copy(
            src_ref=landed,
            dst_ref=landed,
            send_sem=slot_send.at[phase],
            recv_sem=slot_recv.at[phase],
            device_id=peer_at(names, offsets[0]),
            device_id_type=MESH,
        )
        everything.wait_recv()
        slot_copies.append(everything)
        terms = [slots[base + n] for n in range(len(offsets) + 1)]
        while len(terms) > 1:
            terms = [sum(terms[j + 1 : j + 2], terms[j]) for j in range(0, len(terms), 2)]
        value = terms[0]
        base += len(offsets) + 1
    gram_ref[...] = value

    for copy in slot_copies:
        copy.wait_send()
    for copy in x_copies.values():
        copy.wait_send()
    for copy in z_copies.values():
        copy.wait_send()


def gram_call(axes, scale, velocity, weights):
    _, snaps, cells_x, cells_z, cells_y = velocity.shape
    size = snaps * cells_z
    held = jax.ShapeDtypeStruct((3, cells_x, size, cells_y), BF16)
    dma = pltpu.SemaphoreType.DMA
    dims = dims_of(*axes)
    tiles = sum(len(offsets_of(names, dims)) + 1 for names in PHASES)
    return pl.pallas_call(
        functools.partial(gram_kernel, axes, scale),
        out_shape=(
            jax.ShapeDtypeStruct((8, 128), F32),
            held,
            held,
            jax.ShapeDtypeStruct(weights.shape, F32),
        ),
        in_specs=[pl.BlockSpec(memory_space=pltpu.HBM)] * 2,
        out_specs=(pl.BlockSpec(memory_space=pltpu.VMEM),) * 4,
        scratch_shapes=[
            pltpu.VMEM(velocity.shape, BF16),
            pltpu.VMEM(weights.shape, F32),
            pltpu.VMEM((2, 2, snaps, WIDTH, cells_z, cells_y), BF16),
            pltpu.VMEM((2, snaps, cells_x, cells_z, cells_y), BF16),
            pltpu.VMEM((2, cells_x, size, cells_y), F32),
            pltpu.VMEM((size, 2 * size), BF16),
            pltpu.VMEM((2 * size, size), F32),
            pltpu.VMEM((tiles, 8, 128), F32),
            dma((4,)),
            dma((2, 2)),
            dma((2, 2)),
            dma((2, cells_x // 2, 2)),
            dma((2, cells_x // 2, 2)),
            dma((len(PHASES),)),
            dma((len(PHASES),)),
            pltpu.SemaphoreType.REGULAR((ROUNDS,)),
        ],
        compiler_params=pltpu.CompilerParams(
            collective_id=0, has_side_effects=True, vmem_limit_bytes=28 << 20
        ),
        name="curl_gram",
    )(velocity, weights)


TILE = 8


class Elimination:
    def __init__(self, gram):
        snaps, lanes = gram.shape
        self.full = (TILE, lanes)
        lane = iota(self.full, 1)
        self.row = iota(self.full, 0)
        self.inside = (lane >= snaps) & (lane < 2 * snaps)
        self.work = []
        for t in range(snaps // TILE):
            unit = jnp.where(lane == self.row + snaps + t * TILE, 1.0, 0.0)
            self.work.append(jnp.where(lane < snaps, gram[t * TILE : (t + 1) * TILE], unit))
        self.pivots = [jnp.ones(self.full, F32) for _ in self.work]

    def sweep(self, home, between):
        work, full = self.work, self.full
        steps = range(TILE)
        rows = [jnp.broadcast_to(work[home][j : j + 1], full) for j in steps]
        columns = []
        for j in steps:
            k = home * TILE + j
            columns.append(
                {t: jnp.broadcast_to(work[t][:, k : k + 1], full) for t in range(home, len(work))}
            )
        cross = [
            [jnp.broadcast_to(columns[j][home][i : i + 1], full) for j in steps] for i in steps
        ]
        for j in steps:
            pivot = cross[j][j]
            inverse = 1.0 / pivot
            self.pivots[home] = jnp.where(self.row == j, pivot, self.pivots[home])
            factors = {t: columns[j][t] * inverse for t in columns[j]}
            factors[home] = jnp.where(self.row > j, factors[home], 0.0)
            for m in steps[j + 1 :]:
                for t in columns[m]:
                    columns[m][t] = columns[m][t] - factors[t] * cross[j][m]
            for i in steps[j + 1 :]:
                ratio = cross[i][j] * inverse
                rows[i] = rows[i] - ratio * rows[j]
                for m in steps[j + 1 :]:
                    cross[i][m] = cross[i][m] - ratio * cross[j][m]
            for t in columns[j]:
                work[t] = work[t] - factors[t] * rows[j]
            between()

    def rows_of(self, tiles):
        return jnp.concatenate(
            [
                jnp.where(self.inside, self.work[t] / jnp.sqrt(self.pivots[t]), 0.0)
                for t in tiles
            ],
            axis=0,
        )


def mix_kernel(gram_ref, unscale, high, low, out_hbm, out, out_sem):
    _, cells_x, size, cells_y = high.shape
    snaps = out.shape[1]
    cells_z = size // snaps
    half = size // 2

    packed = gram_ref[...]
    lanes = packed.shape[1]
    pieces = [packed] + [
        pltpu.roll(packed, lanes - q * snaps, 1) for q in range(1, lanes // snaps)
    ]
    part = jnp.concatenate(pieces, axis=0)
    part = jnp.where(iota(part.shape, 1) < snaps, part, 0.0)
    tall = jnp.concatenate([part, jnp.zeros((lanes - snaps, lanes), F32)], axis=0)
    work = Elimination(part + tall.T[:snaps])

    ahead = iota((lanes, size), 1) - cells_z * (iota((lanes, size), 0) - snaps)
    spread = ((ahead >= 0) & (ahead < cells_z)).astype(BF16)
    match = iota((cells_z, size), 0) == iota((cells_z, size), 1) & (cells_z - 1)

    def blocks(rows, columns):
        top = rows.astype(BF16)
        rest = (rows - top.astype(F32)).astype(BF16)
        spans = dot_nn(jnp.concatenate([top, rest], axis=0), spread[:, :columns])
        cube = (2 * rows.shape[0], cells_z, columns)
        wide = jnp.where(match[None, :, :columns], jnp.broadcast_to(spans[:, None], cube), 0.0)
        return wide.reshape(-1, columns).astype(BF16)

    pairs = [(c, first) for c in range(3) for first in range(0, cells_x, 2)]
    stores = []

    def sides(ref, c, first, rows):
        return jnp.concatenate([ref[c, first + n, :rows] for n in range(2)], axis=1)

    def put(c, first, begin, mixed):
        count = mixed.shape[0] // cells_z
        for n in range(2):
            cut = mixed[:, n * cells_y : (n + 1) * cells_y]
            cut = cut.reshape(count, cells_z, cells_y) * unscale[first + n][None]
            out[c, begin : begin + count, first + n] = cut

    def send(where, semaphore):
        copy = pltpu.make_async_copy(out.at[where], out_hbm.at[where], semaphore)
        copy.start()
        stores.append(copy)

    for home in range(2):
        work.sweep(home, lambda: None)
    first_rows = blocks(work.rows_of((0, 1)), half)
    twice = jnp.concatenate([first_rows[:half]] * 2, axis=1)
    todo = list(pairs)

    def early():
        if todo:
            c, first = todo.pop(0)
            a, b = sides(high, c, first, half), sides(low, c, first, half)
            mixed = dot_nn(twice, jnp.concatenate([a, b], axis=0)) + dot_nn(first_rows[half:], a)
            put(c, first, 0, mixed)
            if first + 2 == cells_x:
                send((c, pl.ds(0, snaps // 2)), out_sem.at[0, c])

    for home in range(2, 4):
        work.sweep(home, early)
    while todo:
        early()
    second_rows = blocks(work.rows_of((2, 3)), size)
    for n, (c, first) in enumerate(pairs):
        mixed = dot_nn(second_rows, sides(high, c, first, size))
        mixed = mixed[:half] + mixed[half:]
        mixed += dot_nn(second_rows[:half], sides(low, c, first, size))
        put(c, first, snaps // 2, mixed)
        send((c, pl.ds(snaps // 2, snaps // 2), pl.ds(first, 2)), out_sem.at[1, n])
    for copy in stores:
        copy.wait()


def mix_call(shape, gram, unscale, high, low):
    return pl.pallas_call(
        mix_kernel,
        out_shape=jax.ShapeDtypeStruct(shape, F32),
        in_specs=[pl.BlockSpec(memory_space=pltpu.VMEM)] * 4,
        out_specs=pl.BlockSpec(memory_space=pltpu.HBM),
        scratch_shapes=[
            pltpu.VMEM(shape, F32),
            pltpu.SemaphoreType.DMA((2, 3 * shape[2] // 2)),
        ],
        compiler_params=pltpu.CompilerParams(vmem_limit_bytes=28 << 20),
        name="mix",
    )(gram, unscale, high, low)


def solution(mesh):
    placed = (P(None, None, "gx", "gz", None), P("gx", "gz", None))
    axes = (mesh.shape["gx"], mesh.shape["gz"])

    def per_device(velocity, weights):
        rows_all = 3 * weights.size * axes[0] * axes[1]
        scale = float(rows_all) ** 0.5
        velocity, weights = (
            pltpu.with_memory_space_constraint(a, pltpu.HBM) for a in (velocity, weights)
        )
        gram, high, low, unscale = gram_call(axes, scale, velocity, weights)
        return mix_call(velocity.shape, gram, unscale, high, low)

    return jax.shard_map(
        per_device,
        mesh=mesh,
        in_specs=placed,
        out_specs=P(None, None, "gx", "gz", None),
        check_vma=False,
    )
```

```python
import functools
import itertools

import jax
import jax.numpy as jnp
from jax import lax
from jax.experimental import pallas as pl
from jax.experimental.pallas import tpu as pltpu
from jax.sharding import PartitionSpec as P

WHOLE = 840.0
COEFS = (672.0, -168.0, 32.0, -3.0)
WIDTH = len(COEFS)
MESH = pl.DeviceIdType.MESH
F32 = jnp.float32
BF16 = jnp.bfloat16
PAIR = 2
U, V, W = 0, 1, 2


def dims_of(count_x, count_z):
    core = 2
    x = 4 if count_x % 8 == 0 else 1
    return {"y": count_x // (core * x), "x": x, "core": core, "z": count_z}


PHASES = (("z", "core"), ("y", "x"))
ROUNDS = 8


def offsets_of(names, dims):
    def hops(offset):
        return sum(
            min(d, dims[n] - d) * (0.1 if n == "core" else 1.0)
            for n, d in zip(names, offset, strict=True)
        )

    every = itertools.product(*[range(dims[n]) for n in names])
    return sorted((o for o in every if any(o)), key=lambda o: -hops(o))


def dot_nt(a, b):
    return lax.dot_general(a, b, (((1,), (1,)), ((), ())), preferred_element_type=F32)


def dot_nn(a, b):
    return lax.dot_general(a, b, (((1,), (0,)), ((), ())), preferred_element_type=F32)


def stencil(distance):
    total = jnp.zeros(distance.shape, F32)
    for step, weight in enumerate(COEFS, start=1):
        total = jnp.where(distance == step, weight, total)
        total = jnp.where(distance == -step, -weight, total)
    return total


def iota(shape, dim):
    return lax.broadcasted_iota(jnp.int32, shape, dim)


def gram_kernel(
    axes,
    scale,
    vel_hbm,
    weights_hbm,
    gram_ref,
    high,
    low,
    unscale,
    vel,
    weights,
    halo_x,
    halo_z,
    part,
    span_matrix,
    acc,
    slots,
    vel_sem,
    x_send,
    x_recv,
    z_send,
    z_recv,
    slot_send,
    slot_recv,
    news,
):
    snaps, cells_x, cells_z, cells_y = vel_hbm.shape[1:]
    size = snaps * cells_z
    count_x, count_z = axes
    dims = dims_of(count_x, count_z)
    gx, gz = lax.axis_index("gx"), lax.axis_index("gz")
    core_x = dims["x"] * dims["core"]
    mine = {
        "y": gx // core_x,
        "x": lax.rem(gx // dims["core"], dims["x"]),
        "core": lax.rem(gx, dims["core"]),
        "z": gz,
    }

    def peer_at(names, offset):
        place = dict(mine)
        for name, d in zip(names, offset, strict=True):
            if d:
                place[name] = lax.rem(place[name] + d, dims[name])
        return (place["y"] * core_x + place["x"] * dims["core"] + place["core"], place["z"])

    right_x, left_x = lax.rem(gx + 1, count_x), lax.rem(gx + count_x - 1, count_x)
    right_z, left_z = lax.rem(gz + 1, count_z), lax.rem(gz + count_z - 1, count_z)

    def beside(*names):
        return [
            peer_at((name,), (step,)) for name in names for step in (1, dims[name] - 1) if step
        ]

    def signal(semaphore, peers):
        for peer in peers:
            pl.semaphore_signal(semaphore, inc=1, device_id=peer, device_id_type=MESH)

    barrier = pltpu.get_barrier_semaphore()
    direct = [(right_x, gz), (left_x, gz)] + beside("z", "y", "x")
    signal(barrier, direct)
    rounds = [beside("x")] * max(dims["x"] // 2 - 1, 0)
    rounds += [beside("z", "y")] * max(dims["z"] // 2, dims["y"] // 2)
    heard = [0]

    def tell():
        if heard[0] < len(rounds):
            signal(news.at[heard[0]], rounds[heard[0]])

    def hear():
        if heard[0] < len(rounds):
            pl.semaphore_wait(news.at[heard[0]], len(rounds[heard[0]]))
            heard[0] += 1
            tell()

    loads = [
        pltpu.make_async_copy(vel_hbm.at[c], vel.at[c], vel_sem.at[c]) for c in (W, U, V)
    ]
    loads.append(pltpu.make_async_copy(weights_hbm, weights, vel_sem.at[3]))
    for load in loads:
        load.start()

    pl.semaphore_wait(barrier, len(direct))

    z_copies = {}
    x_copies = {}
    twos = [(first, 2) for first in range(0, cells_x, 2)]
    chunks = ([(0, 4), (4, 4)], [(0, 4), (4, 2), (6, 2)])

    def start_z(k):
        source = (V, U)[k]
        for first, count in chunks[k]:
            xs = pl.ds(first, count)
            for side, peer in ((0, (gx, left_z)), (1, (gx, right_z))):
                rows = pl.ds(side * WIDTH, WIDTH)
                copy = pltpu.make_async_remote_copy(
                    src_ref=vel_hbm.at[source, :, xs, rows, :],
                    dst_ref=halo_z.at[k, :, xs, rows, :],
                    send_sem=z_send.at[k, first, side],
                    recv_sem=z_recv.at[k, first, side],
                    device_id=peer,
                    device_id_type=MESH,
                )
                copy.start()
                z_copies[k, first, side] = copy

    def start_x():
        for k, source in enumerate((V, W)):
            for side, peer, first in ((0, (right_x, gz), cells_x - WIDTH), (1, (left_x, gz), 0)):
                copy = pltpu.make_async_remote_copy(
                    src_ref=vel_hbm.at[source, :, pl.ds(first, WIDTH)],
                    dst_ref=halo_x.at[k, side],
                    send_sem=x_send.at[k, side],
                    recv_sem=x_recv.at[k, side],
                    device_id=peer,
                    device_id_type=MESH,
                )
                copy.start()
                x_copies[k, side] = copy

    start_z(0)
    start_x()
    start_z(1)
    tell()

    wall = stencil(iota((cells_y, cells_y), 0) - iota((cells_y, cells_y), 1)).astype(BF16)
    wide = (size, size)
    to_row, from_row = iota(wide, 0), iota(wide, 1)
    to_z, from_z = to_row & (cells_z - 1), from_row & (cells_z - 1)
    same = to_row - to_z == from_row - from_z
    beyond = jnp.where(from_z < WIDTH, from_z + cells_z, from_z - cells_z)
    for n, source_z in enumerate((from_z, beyond)):
        span_matrix[:, n * size : (n + 1) * size] = jnp.where(
            same, stencil(source_z - to_z), 0.0
        ).astype(BF16)

    hear()
    for load in loads:
        load.wait()

    root_weights = jnp.sqrt(weights[...])
    root = root_weights * (1.0 / WHOLE)
    unscale[...] = scale / root_weights

    def plane_of(ref, c, x):
        return ref[c, :, x].reshape(size, cells_y)

    @pl.loop(0, cells_x)
    def _(x):
        both = jnp.concatenate([plane_of(vel, W, x), plane_of(vel, U, x)], axis=0)
        part[pl.ds(0, 2), x] = dot_nn(both, wall).reshape(2, size, cells_y)

    def keep(c, x, rows, value):
        scaled = (value.reshape(-1, cells_z, cells_y) * root[x][None]).reshape(value.shape)
        rounded = scaled.astype(BF16)
        high[c, x, rows, :] = rounded
        low[c, x, rows, :] = (scaled - rounded.astype(F32)).astype(BF16)

    def product(c, first, count):
        tops = jnp.concatenate([high[c, first + x] for x in range(count)], axis=1)
        rests = jnp.concatenate([low[c, first + x] for x in range(count)], axis=1)
        return dot_nt(jnp.concatenate([tops, rests], axis=0), tops)

    rows_pair = PAIR * cells_z

    def stream(k, i):
        pair = pl.ds(i * PAIR, PAIR)
        ext = jnp.concatenate(
            [
                halo_x[k, 0, pair].astype(F32),
                vel[(V, W)[k], pair].astype(F32),
                halo_x[k, 1, pair].astype(F32),
            ],
            axis=1,
        )
        for x in range(cells_x):
            total = None
            for step, weight in enumerate(COEFS, start=1):
                term = weight * (ext[:, WIDTH + x + step] - ext[:, WIDTH + x - step])
                total = term if total is None else total + term
            yield x, total.reshape(rows_pair, cells_y)

    hear()
    for side in range(2):
        x_copies[0, side].wait_recv()

    @pl.loop(0, snaps // PAIR)
    def _(i):
        rows = pl.ds(pl.multiple_of(i * rows_pair, rows_pair), rows_pair)
        for x, value in stream(0, i):
            keep(2, x, rows, value - part[1, x, rows])

    hear()
    for side in range(2):
        x_copies[1, side].wait_recv()

    @pl.loop(0, snaps // PAIR)
    def _(i):
        rows = pl.ds(pl.multiple_of(i * rows_pair, rows_pair), rows_pair)
        for x, value in stream(1, i):
            part[1, x, rows] = value

    hear()
    acc[...] = product(2, 0, cells_x // 2)
    acc[...] += product(2, cells_x // 2, cells_x // 2)

    for k, source in enumerate((V, U)):
        for first, count in chunks[k]:
            for side in range(2):
                z_copies[k, first, side].wait_recv()
            xs = range(first, first + count)
            inner = jnp.concatenate([plane_of(vel, source, x) for x in xs], axis=1)
            outer = jnp.concatenate([plane_of(halo_z, k, x) for x in xs], axis=1)
            span = dot_nn(span_matrix[...], jnp.concatenate([inner, outer], axis=0))
            for n, x in enumerate(xs):
                cut = span[:, n * cells_y : (n + 1) * cells_y]
                keep(k, x, slice(None), part[0, x] - cut if k == 0 else cut - part[1, x])
            if (k, first, count) != (1, *chunks[1][-1]):
                acc[...] += product(k, first, count)
        if k == 0:
            for _ in range(len(rounds)):
                hear()

    square = acc[...] + product(1, *chunks[1][-1])
    square = (0.5 * square[:size] + square[size:]).reshape(snaps, cells_z, size)
    match = iota((cells_z, size), 0) == iota((cells_z, size), 1) & (cells_z - 1)
    matched = jnp.where(match[None], square, 0.0).sum(axis=1)
    per_row, lanes = gram_ref.shape
    ahead = iota((size, lanes), 0) - cells_z * iota((size, lanes), 1)
    gather = ((ahead >= 0) & (ahead < cells_z)).astype(BF16)
    one = matched.astype(BF16)
    rest = matched - one.astype(F32)
    two = rest.astype(BF16)
    three = (rest - two.astype(F32)).astype(BF16)
    half = dot_nn(jnp.concatenate([one, two, three], axis=0), gather)
    half = half[:snaps] + half[snaps : 2 * snaps] + half[2 * snaps :]
    packed = half[:per_row]
    for q in range(1, snaps // per_row):
        packed += pltpu.roll(half[q * per_row : (q + 1) * per_row], q * snaps, 1)

    slot_copies = []
    value = packed
    base = 0
    for phase, names in enumerate(PHASES):
        offsets = offsets_of(names, dims)
        slots[base] = value
        for n, offset in enumerate(offsets, start=1):
            pltpu.make_async_remote_copy(
                src_ref=slots.at[base],
                dst_ref=slots.at[base + n],
                send_sem=slot_send.at[phase],
                recv_sem=slot_recv.at[phase],
                device_id=peer_at(names, offset),
                device_id_type=MESH,
            ).start()
        landed = slots.at[pl.ds(base + 1, len(offsets))]
        everything = pltpu.make_async_remote_copy(
            src_ref=landed,
            dst_ref=landed,
            send_sem=slot_send.at[phase],
            recv_sem=slot_recv.at[phase],
            device_id=peer_at(names, offsets[0]),
            device_id_type=MESH,
        )
        everything.wait_recv()
        slot_copies.append(everything)
        terms = [slots[base + n] for n in range(len(offsets) + 1)]
        while len(terms) > 1:
            terms = [sum(terms[j + 1 : j + 2], terms[j]) for j in range(0, len(terms), 2)]
        value = terms[0]
        base += len(offsets) + 1
    gram_ref[...] = value

    for copy in slot_copies:
        copy.wait_send()
    for copy in x_copies.values():
        copy.wait_send()
    for copy in z_copies.values():
        copy.wait_send()


def gram_call(axes, scale, velocity, weights):
    _, snaps, cells_x, cells_z, cells_y = velocity.shape
    size = snaps * cells_z
    held = jax.ShapeDtypeStruct((3, cells_x, size, cells_y), BF16)
    dma = pltpu.SemaphoreType.DMA
    dims = dims_of(*axes)
    tiles = sum(len(offsets_of(names, dims)) + 1 for names in PHASES)
    return pl.pallas_call(
        functools.partial(gram_kernel, axes, scale),
        out_shape=(
            jax.ShapeDtypeStruct((8, 128), F32),
            held,
            held,
            jax.ShapeDtypeStruct(weights.shape, F32),
        ),
        in_specs=[pl.BlockSpec(memory_space=pltpu.HBM)] * 2,
        out_specs=(pl.BlockSpec(memory_space=pltpu.VMEM),) * 4,
        scratch_shapes=[
            pltpu.VMEM(velocity.shape, BF16),
            pltpu.VMEM(weights.shape, F32),
            pltpu.VMEM((2, 2, snaps, WIDTH, cells_z, cells_y), BF16),
            pltpu.VMEM((2, snaps, cells_x, cells_z, cells_y), BF16),
            pltpu.VMEM((2, cells_x, size, cells_y), F32),
            pltpu.VMEM((size, 2 * size), BF16),
            pltpu.VMEM((2 * size, size), F32),
            pltpu.VMEM((tiles, 8, 128), F32),
            dma((4,)),
            dma((2, 2)),
            dma((2, 2)),
            dma((2, cells_x, 2)),
            dma((2, cells_x, 2)),
            dma((len(PHASES),)),
            dma((len(PHASES),)),
            pltpu.SemaphoreType.REGULAR((ROUNDS,)),
        ],
        compiler_params=pltpu.CompilerParams(
            collective_id=0, has_side_effects=True, vmem_limit_bytes=28 << 20
        ),
        name="curl_gram",
    )(velocity, weights)


TILE = 8


class Elimination:
    def __init__(self, gram):
        snaps, lanes = gram.shape
        self.full = (TILE, lanes)
        lane = iota(self.full, 1)
        self.row = iota(self.full, 0)
        self.inside = (lane >= snaps) & (lane < 2 * snaps)
        self.work = []
        for t in range(snaps // TILE):
            unit = jnp.where(lane == self.row + snaps + t * TILE, 1.0, 0.0)
            self.work.append(jnp.where(lane < snaps, gram[t * TILE : (t + 1) * TILE], unit))
        self.pivots = [jnp.ones(self.full, F32) for _ in self.work]

    def sweep(self, home, between):
        work, full = self.work, self.full
        steps = range(TILE)
        rows = [jnp.broadcast_to(work[home][j : j + 1], full) for j in steps]
        columns = []
        for j in steps:
            k = home * TILE + j
            columns.append(
                {t: jnp.broadcast_to(work[t][:, k : k + 1], full) for t in range(home, len(work))}
            )
        cross = [
            [jnp.broadcast_to(columns[j][home][i : i + 1], full) for j in steps] for i in steps
        ]
        for j in steps:
            pivot = cross[j][j]
            inverse = 1.0 / pivot
            self.pivots[home] = jnp.where(self.row == j, pivot, self.pivots[home])
            factors = {t: columns[j][t] * inverse for t in columns[j]}
            factors[home] = jnp.where(self.row > j, factors[home], 0.0)
            for m in steps[j + 1 :]:
                for t in columns[m]:
                    columns[m][t] = columns[m][t] - factors[t] * cross[j][m]
            for i in steps[j + 1 :]:
                ratio = cross[i][j] * inverse
                rows[i] = rows[i] - ratio * rows[j]
                for m in steps[j + 1 :]:
                    cross[i][m] = cross[i][m] - ratio * cross[j][m]
            for t in columns[j]:
                work[t] = work[t] - factors[t] * rows[j]
            between()

    def rows_of(self, tiles):
        return jnp.concatenate(
            [
                jnp.where(self.inside, self.work[t] / jnp.sqrt(self.pivots[t]), 0.0)
                for t in tiles
            ],
            axis=0,
        )


def mix_kernel(gram_ref, unscale, high, low, out_hbm, out, out_sem):
    _, cells_x, size, cells_y = high.shape
    snaps = out.shape[1]
    cells_z = size // snaps
    half = size // 2

    packed = gram_ref[...]
    lanes = packed.shape[1]
    pieces = [packed] + [
        pltpu.roll(packed, lanes - q * snaps, 1) for q in range(1, lanes // snaps)
    ]
    part = jnp.concatenate(pieces, axis=0)
    part = jnp.where(iota(part.shape, 1) < snaps, part, 0.0)
    tall = jnp.concatenate([part, jnp.zeros((lanes - snaps, lanes), F32)], axis=0)
    work = Elimination(part + tall.T[:snaps])

    ahead = iota((lanes, size), 1) - cells_z * (iota((lanes, size), 0) - snaps)
    spread = ((ahead >= 0) & (ahead < cells_z)).astype(BF16)
    match = iota((cells_z, size), 0) == iota((cells_z, size), 1) & (cells_z - 1)

    def blocks(rows, columns):
        top = rows.astype(BF16)
        rest = (rows - top.astype(F32)).astype(BF16)
        spans = dot_nn(jnp.concatenate([top, rest], axis=0), spread[:, :columns])
        cube = (2 * rows.shape[0], cells_z, columns)
        wide = jnp.where(match[None, :, :columns], jnp.broadcast_to(spans[:, None], cube), 0.0)
        return wide.reshape(-1, columns).astype(BF16)

    pairs = [(c, first) for c in range(3) for first in range(0, cells_x, 2)]
    stores = []

    def sides(ref, c, first, rows):
        return jnp.concatenate([ref[c, first + n, :rows] for n in range(2)], axis=1)

    def put(c, first, begin, mixed):
        count = mixed.shape[0] // cells_z
        for n in range(2):
            cut = mixed[:, n * cells_y : (n + 1) * cells_y]
            cut = cut.reshape(count, cells_z, cells_y) * unscale[first + n][None]
            out[c, begin : begin + count, first + n] = cut

    def send(where, semaphore):
        copy = pltpu.make_async_copy(out.at[where], out_hbm.at[where], semaphore)
        copy.start()
        stores.append(copy)

    for home in range(2):
        work.sweep(home, lambda: None)
    first_rows = blocks(work.rows_of((0, 1)), half)
    twice = jnp.concatenate([first_rows[:half]] * 2, axis=1)
    todo = list(pairs)

    def early():
        if todo:
            c, first = todo.pop(0)
            a, b = sides(high, c, first, half), sides(low, c, first, half)
            mixed = dot_nn(twice, jnp.concatenate([a, b], axis=0)) + dot_nn(first_rows[half:], a)
            put(c, first, 0, mixed)
            if first + 2 == cells_x:
                send((c, pl.ds(0, snaps // 2)), out_sem.at[0, c])

    for home in range(2, 4):
        work.sweep(home, early)
    while todo:
        early()
    second_rows = blocks(work.rows_of((2, 3)), size)
    for n, (c, first) in enumerate(pairs):
        mixed = dot_nn(second_rows, sides(high, c, first, size))
        mixed = mixed[:half] + mixed[half:]
        mixed += dot_nn(second_rows[:half], sides(low, c, first, size))
        put(c, first, snaps // 2, mixed)
        send((c, pl.ds(snaps // 2, snaps // 2), pl.ds(first, 2)), out_sem.at[1, n])
    for copy in stores:
        copy.wait()


def mix_call(shape, gram, unscale, high, low):
    return pl.pallas_call(
        mix_kernel,
        out_shape=jax.ShapeDtypeStruct(shape, F32),
        in_specs=[pl.BlockSpec(memory_space=pltpu.VMEM)] * 4,
        out_specs=pl.BlockSpec(memory_space=pltpu.HBM),
        scratch_shapes=[
            pltpu.VMEM(shape, F32),
            pltpu.SemaphoreType.DMA((2, 3 * shape[2] // 2)),
        ],
        compiler_params=pltpu.CompilerParams(vmem_limit_bytes=28 << 20),
        name="mix",
    )(gram, unscale, high, low)


def solution(mesh):
    placed = (P(None, None, "gx", "gz", None), P("gx", "gz", None))
    axes = (mesh.shape["gx"], mesh.shape["gz"])

    def per_device(velocity, weights):
        rows_all = 3 * weights.size * axes[0] * axes[1]
        scale = float(rows_all) ** 0.5
        velocity, weights = (
            pltpu.with_memory_space_constraint(a, pltpu.HBM) for a in (velocity, weights)
        )
        gram, high, low, unscale = gram_call(axes, scale, velocity, weights)
        return mix_call(velocity.shape, gram, unscale, high, low)

    return jax.shard_map(
        per_device,
        mesh=mesh,
        in_specs=placed,
        out_specs=P(None, None, "gx", "gz", None),
        check_vma=False,
    )
```

```python
import functools
import itertools

import jax
import jax.numpy as jnp
from jax import lax
from jax.experimental import pallas as pl
from jax.experimental.pallas import tpu as pltpu
from jax.sharding import PartitionSpec as P

WHOLE = 840.0
COEFS = (672.0, -168.0, 32.0, -3.0)
WIDTH = len(COEFS)
MESH = pl.DeviceIdType.MESH
F32 = jnp.float32
BF16 = jnp.bfloat16
PAIR = 2
U, V, W = 0, 1, 2


def dims_of(count_x, count_z):
    core = 2
    x = 4 if count_x % 8 == 0 else 1
    return {"y": count_x // (core * x), "x": x, "core": core, "z": count_z}


PHASES = (("z", "core"), ("y", "x"))
ROUNDS = 8


def offsets_of(names, dims):
    def hops(offset):
        return sum(
            min(d, dims[n] - d) * (0.1 if n == "core" else 1.0)
            for n, d in zip(names, offset, strict=True)
        )

    every = itertools.product(*[range(dims[n]) for n in names])
    return sorted((o for o in every if any(o)), key=lambda o: -hops(o))


def dot_nt(a, b):
    return lax.dot_general(a, b, (((1,), (1,)), ((), ())), preferred_element_type=F32)


def dot_nn(a, b):
    return lax.dot_general(a, b, (((1,), (0,)), ((), ())), preferred_element_type=F32)


def stencil(distance):
    total = jnp.zeros(distance.shape, F32)
    for step, weight in enumerate(COEFS, start=1):
        total = jnp.where(distance == step, weight, total)
        total = jnp.where(distance == -step, -weight, total)
    return total


def iota(shape, dim):
    return lax.broadcasted_iota(jnp.int32, shape, dim)


def gram_kernel(
    axes,
    scale,
    vel_hbm,
    weights_hbm,
    gram_ref,
    high,
    low,
    unscale,
    vel,
    weights,
    halo_x,
    halo_z,
    part,
    span_matrix,
    acc,
    gather,
    slots,
    vel_sem,
    x_send,
    x_recv,
    z_send,
    z_recv,
    slot_send,
    slot_recv,
    news,
):
    snaps, cells_x, cells_z, cells_y = vel_hbm.shape[1:]
    size = snaps * cells_z
    count_x, count_z = axes
    dims = dims_of(count_x, count_z)
    gx, gz = lax.axis_index("gx"), lax.axis_index("gz")
    core_x = dims["x"] * dims["core"]
    mine = {
        "y": gx // core_x,
        "x": lax.rem(gx // dims["core"], dims["x"]),
        "core": lax.rem(gx, dims["core"]),
        "z": gz,
    }

    def peer_at(names, offset):
        place = dict(mine)
        for name, d in zip(names, offset, strict=True):
            if d:
                place[name] = lax.rem(place[name] + d, dims[name])
        return (place["y"] * core_x + place["x"] * dims["core"] + place["core"], place["z"])

    right_x, left_x = lax.rem(gx + 1, count_x), lax.rem(gx + count_x - 1, count_x)
    right_z, left_z = lax.rem(gz + 1, count_z), lax.rem(gz + count_z - 1, count_z)

    def beside(*names):
        return [
            peer_at((name,), (step,)) for name in names for step in (1, dims[name] - 1) if step
        ]

    def signal(semaphore, peers):
        for peer in peers:
            pl.semaphore_signal(semaphore, inc=1, device_id=peer, device_id_type=MESH)

    barrier = pltpu.get_barrier_semaphore()
    direct = [(right_x, gz), (left_x, gz)] + beside("z", "y", "x")
    signal(barrier, direct)
    rounds = [beside("x")] * max(dims["x"] // 2 - 1, 0)
    rounds += [beside("z", "y")] * max(dims["z"] // 2, dims["y"] // 2)
    heard = [0]

    def tell():
        if heard[0] < len(rounds):
            signal(news.at[heard[0]], rounds[heard[0]])

    def hear():
        if heard[0] < len(rounds):
            pl.semaphore_wait(news.at[heard[0]], len(rounds[heard[0]]))
            heard[0] += 1
            tell()

    loads = [
        pltpu.make_async_copy(vel_hbm.at[c], vel.at[c], vel_sem.at[c]) for c in (W, U, V)
    ]
    loads.append(pltpu.make_async_copy(weights_hbm, weights, vel_sem.at[3]))
    for load in loads:
        load.start()

    pl.semaphore_wait(barrier, len(direct))

    z_copies = {}
    x_copies = {}
    twos = [(first, 2) for first in range(0, cells_x, 2)]
    chunks = ([(0, 4), (4, 4)], [(0, 4), (4, 2), (6, 2)])

    def start_z(k):
        source = (V, U)[k]
        for first, count in chunks[k]:
            xs = pl.ds(first, count)
            for side, peer in ((0, (gx, left_z)), (1, (gx, right_z))):
                rows = pl.ds(side * WIDTH, WIDTH)
                copy = pltpu.make_async_remote_copy(
                    src_ref=vel_hbm.at[source, :, xs, rows, :],
                    dst_ref=halo_z.at[k, :, xs, rows, :],
                    send_sem=z_send.at[k, first, side],
                    recv_sem=z_recv.at[k, first, side],
                    device_id=peer,
                    device_id_type=MESH,
                )
                copy.start()
                z_copies[k, first, side] = copy

    def start_x():
        for k, source in enumerate((V, W)):
            for side, peer, first in ((0, (right_x, gz), cells_x - WIDTH), (1, (left_x, gz), 0)):
                copy = pltpu.make_async_remote_copy(
                    src_ref=vel_hbm.at[source, :, pl.ds(first, WIDTH)],
                    dst_ref=halo_x.at[k, side],
                    send_sem=x_send.at[k, side],
                    recv_sem=x_recv.at[k, side],
                    device_id=peer,
                    device_id_type=MESH,
                )
                copy.start()
                x_copies[k, side] = copy

    start_z(0)
    start_x()
    start_z(1)
    tell()

    wall = stencil(iota((cells_y, cells_y), 0) - iota((cells_y, cells_y), 1)).astype(BF16)
    wide = (size, size)
    to_row, from_row = iota(wide, 0), iota(wide, 1)
    to_z, from_z = to_row & (cells_z - 1), from_row & (cells_z - 1)
    same = to_row - to_z == from_row - from_z
    beyond = jnp.where(from_z < WIDTH, from_z + cells_z, from_z - cells_z)
    for n, source_z in enumerate((from_z, beyond)):
        span_matrix[:, n * size : (n + 1) * size] = jnp.where(
            same, stencil(source_z - to_z), 0.0
        ).astype(BF16)

    hear()
    for load in loads:
        load.wait()

    root_weights = jnp.sqrt(weights[...])
    root = root_weights * (1.0 / WHOLE)
    unscale[...] = scale / root_weights

    def plane_of(ref, c, x):
        return ref[c, :, x].reshape(size, cells_y)

    @pl.loop(0, cells_x)
    def _(x):
        both = jnp.concatenate([plane_of(vel, W, x), plane_of(vel, U, x)], axis=0)
        part[pl.ds(0, 2), x] = dot_nn(both, wall).reshape(2, size, cells_y)

    def keep(c, x, rows, value):
        scaled = (value.reshape(-1, cells_z, cells_y) * root[x][None]).reshape(value.shape)
        top = scaled.astype(BF16)
        rest = (scaled - top.astype(F32)).astype(BF16)
        high[c, x, rows, :] = top
        low[c, x, rows, :] = rest
        return top, rest

    def product(planes):
        tops, rests = (jnp.concatenate(side, axis=1) for side in zip(*planes, strict=True))
        return dot_nt(jnp.concatenate([tops, rests], axis=0), tops)

    rows_pair = PAIR * cells_z

    def stream(k, i):
        pair = pl.ds(i * PAIR, PAIR)
        ext = jnp.concatenate(
            [
                halo_x[k, 0, pair].astype(F32),
                vel[(V, W)[k], pair].astype(F32),
                halo_x[k, 1, pair].astype(F32),
            ],
            axis=1,
        )
        for x in range(cells_x):
            total = None
            for step, weight in enumerate(COEFS, start=1):
                term = weight * (ext[:, WIDTH + x + step] - ext[:, WIDTH + x - step])
                total = term if total is None else total + term
            yield x, total.reshape(rows_pair, cells_y)

    hear()
    for side in range(2):
        x_copies[0, side].wait_recv()

    @pl.loop(0, snaps // PAIR)
    def _(i):
        rows = pl.ds(pl.multiple_of(i * rows_pair, rows_pair), rows_pair)
        for x, value in stream(0, i):
            keep(2, x, rows, value - part[1, x, rows])

    hear()
    for side in range(2):
        x_copies[1, side].wait_recv()

    @pl.loop(0, snaps // PAIR)
    def _(i):
        rows = pl.ds(pl.multiple_of(i * rows_pair, rows_pair), rows_pair)
        for x, value in stream(1, i):
            part[1, x, rows] = value

    hear()
    kept = [(high[2, x], low[2, x]) for x in range(cells_x)]
    acc[...] = product(kept[: cells_x // 2])
    acc[...] += product(kept[cells_x // 2 :])
    ahead = iota(gather.shape, 0) - cells_z * iota(gather.shape, 1)
    gather[...] = ((ahead >= 0) & (ahead < cells_z)).astype(BF16)

    for k, source in enumerate((V, U)):
        for first, count in chunks[k]:
            for side in range(2):
                z_copies[k, first, side].wait_recv()
            xs = range(first, first + count)
            inner = jnp.concatenate([plane_of(vel, source, x) for x in xs], axis=1)
            outer = jnp.concatenate([plane_of(halo_z, k, x) for x in xs], axis=1)
            span = dot_nn(span_matrix[...], jnp.concatenate([inner, outer], axis=0))
            kept = []
            for n, x in enumerate(xs):
                cut = span[:, n * cells_y : (n + 1) * cells_y]
                value = part[0, x] - cut if k == 0 else cut - part[1, x]
                kept.append(keep(k, x, slice(None), value))
            if (k, first, count) != (1, *chunks[1][-1]):
                acc[...] += product(kept)
        if k == 0:
            for _ in range(len(rounds)):
                hear()

    square = acc[...] + product(kept)
    square = (0.5 * square[:size] + square[size:]).reshape(snaps, cells_z, size)
    match = iota((cells_z, size), 0) == iota((cells_z, size), 1) & (cells_z - 1)
    matched = jnp.where(match[None], square, 0.0).sum(axis=1)
    per_row = gram_ref.shape[0]
    one = matched.astype(BF16)
    rest = matched - one.astype(F32)
    two = rest.astype(BF16)
    three = (rest - two.astype(F32)).astype(BF16)
    half = dot_nn(jnp.concatenate([one, two, three], axis=0), gather[...])
    half = half[:snaps] + half[snaps : 2 * snaps] + half[2 * snaps :]
    packed = half[:per_row]
    for q in range(1, snaps // per_row):
        packed += pltpu.roll(half[q * per_row : (q + 1) * per_row], q * snaps, 1)

    slot_copies = []
    value = packed
    base = 0
    for phase, names in enumerate(PHASES):
        offsets = offsets_of(names, dims)
        slots[base] = value
        for n, offset in enumerate(offsets, start=1):
            pltpu.make_async_remote_copy(
                src_ref=slots.at[base],
                dst_ref=slots.at[base + n],
                send_sem=slot_send.at[phase],
                recv_sem=slot_recv.at[phase],
                device_id=peer_at(names, offset),
                device_id_type=MESH,
            ).start()
        landed = slots.at[pl.ds(base + 1, len(offsets))]
        everything = pltpu.make_async_remote_copy(
            src_ref=landed,
            dst_ref=landed,
            send_sem=slot_send.at[phase],
            recv_sem=slot_recv.at[phase],
            device_id=peer_at(names, offsets[0]),
            device_id_type=MESH,
        )
        everything.wait_recv()
        slot_copies.append(everything)
        terms = [slots[base + n] for n in range(len(offsets) + 1)]
        while len(terms) > 1:
            terms = [sum(terms[j + 1 : j + 2], terms[j]) for j in range(0, len(terms), 2)]
        value = terms[0]
        base += len(offsets) + 1
    gram_ref[...] = value

    for copy in slot_copies:
        copy.wait_send()
    for copy in x_copies.values():
        copy.wait_send()
    for copy in z_copies.values():
        copy.wait_send()


def gram_call(axes, scale, velocity, weights):
    _, snaps, cells_x, cells_z, cells_y = velocity.shape
    size = snaps * cells_z
    held = jax.ShapeDtypeStruct((3, cells_x, size, cells_y), BF16)
    dma = pltpu.SemaphoreType.DMA
    dims = dims_of(*axes)
    tiles = sum(len(offsets_of(names, dims)) + 1 for names in PHASES)
    return pl.pallas_call(
        functools.partial(gram_kernel, axes, scale),
        out_shape=(
            jax.ShapeDtypeStruct((8, 128), F32),
            held,
            held,
            jax.ShapeDtypeStruct(weights.shape, F32),
        ),
        in_specs=[pl.BlockSpec(memory_space=pltpu.HBM)] * 2,
        out_specs=(pl.BlockSpec(memory_space=pltpu.VMEM),) * 4,
        scratch_shapes=[
            pltpu.VMEM(velocity.shape, BF16),
            pltpu.VMEM(weights.shape, F32),
            pltpu.VMEM((2, 2, snaps, WIDTH, cells_z, cells_y), BF16),
            pltpu.VMEM((2, snaps, cells_x, cells_z, cells_y), BF16),
            pltpu.VMEM((2, cells_x, size, cells_y), F32),
            pltpu.VMEM((size, 2 * size), BF16),
            pltpu.VMEM((2 * size, size), F32),
            pltpu.VMEM((size, 128), BF16),
            pltpu.VMEM((tiles, 8, 128), F32),
            dma((4,)),
            dma((2, 2)),
            dma((2, 2)),
            dma((2, cells_x, 2)),
            dma((2, cells_x, 2)),
            dma((len(PHASES),)),
            dma((len(PHASES),)),
            pltpu.SemaphoreType.REGULAR((ROUNDS,)),
        ],
        compiler_params=pltpu.CompilerParams(
            collective_id=0, has_side_effects=True, vmem_limit_bytes=28 << 20
        ),
        name="curl_gram",
    )(velocity, weights)


TILE = 8


class Elimination:
    def __init__(self, gram):
        snaps, lanes = gram.shape
        self.full = (TILE, lanes)
        lane = iota(self.full, 1)
        self.row = iota(self.full, 0)
        self.inside = (lane >= snaps) & (lane < 2 * snaps)
        self.work = []
        for t in range(snaps // TILE):
            unit = jnp.where(lane == self.row + snaps + t * TILE, 1.0, 0.0)
            self.work.append(jnp.where(lane < snaps, gram[t * TILE : (t + 1) * TILE], unit))
        self.pivots = [jnp.ones(self.full, F32) for _ in self.work]

    def sweep(self, home, between):
        work, full = self.work, self.full
        steps = range(TILE)
        rows = [jnp.broadcast_to(work[home][j : j + 1], full) for j in steps]
        columns = []
        for j in steps:
            k = home * TILE + j
            columns.append(
                {t: jnp.broadcast_to(work[t][:, k : k + 1], full) for t in range(home, len(work))}
            )
        cross = [
            [jnp.broadcast_to(columns[j][home][i : i + 1], full) for j in steps] for i in steps
        ]
        for j in steps:
            pivot = cross[j][j]
            inverse = 1.0 / pivot
            self.pivots[home] = jnp.where(self.row == j, pivot, self.pivots[home])
            factors = {t: columns[j][t] * inverse for t in columns[j]}
            factors[home] = jnp.where(self.row > j, factors[home], 0.0)
            for m in steps[j + 1 :]:
                for t in columns[m]:
                    columns[m][t] = columns[m][t] - factors[t] * cross[j][m]
            for i in steps[j + 1 :]:
                ratio = cross[i][j] * inverse
                rows[i] = rows[i] - ratio * rows[j]
                for m in steps[j + 1 :]:
                    cross[i][m] = cross[i][m] - ratio * cross[j][m]
            for t in columns[j]:
                work[t] = work[t] - factors[t] * rows[j]
            between()

    def rows_of(self, tiles):
        return jnp.concatenate(
            [
                jnp.where(self.inside, self.work[t] / jnp.sqrt(self.pivots[t]), 0.0)
                for t in tiles
            ],
            axis=0,
        )


def mix_kernel(gram_ref, unscale, high, low, out_hbm, out, out_sem):
    _, cells_x, size, cells_y = high.shape
    snaps = out.shape[1]
    cells_z = size // snaps
    half = size // 2

    packed = gram_ref[...]
    lanes = packed.shape[1]
    pieces = [packed] + [
        pltpu.roll(packed, lanes - q * snaps, 1) for q in range(1, lanes // snaps)
    ]
    part = jnp.concatenate(pieces, axis=0)
    part = jnp.where(iota(part.shape, 1) < snaps, part, 0.0)
    tall = jnp.concatenate([part, jnp.zeros((lanes - snaps, lanes), F32)], axis=0)
    work = Elimination(part + tall.T[:snaps])

    ahead = iota((lanes, size), 1) - cells_z * (iota((lanes, size), 0) - snaps)
    spread = ((ahead >= 0) & (ahead < cells_z)).astype(BF16)
    match = iota((cells_z, size), 0) == iota((cells_z, size), 1) & (cells_z - 1)

    def blocks(rows, columns):
        top = rows.astype(BF16)
        rest = (rows - top.astype(F32)).astype(BF16)
        spans = dot_nn(jnp.concatenate([top, rest], axis=0), spread[:, :columns])
        cube = (2 * rows.shape[0], cells_z, columns)
        wide = jnp.where(match[None, :, :columns], jnp.broadcast_to(spans[:, None], cube), 0.0)
        return wide.reshape(-1, columns).astype(BF16)

    pairs = [(c, first) for c in range(3) for first in range(0, cells_x, 2)]
    stores = []

    def sides(ref, c, first, rows):
        return jnp.concatenate([ref[c, first + n, :rows] for n in range(2)], axis=1)

    def put(c, first, begin, mixed):
        count = mixed.shape[0] // cells_z
        for n in range(2):
            cut = mixed[:, n * cells_y : (n + 1) * cells_y]
            cut = cut.reshape(count, cells_z, cells_y) * unscale[first + n][None]
            out[c, begin : begin + count, first + n] = cut

    def send(where, semaphore):
        copy = pltpu.make_async_copy(out.at[where], out_hbm.at[where], semaphore)
        copy.start()
        stores.append(copy)

    for home in range(2):
        work.sweep(home, lambda: None)
    first_rows = blocks(work.rows_of((0, 1)), half)
    twice = jnp.concatenate([first_rows[:half]] * 2, axis=1)
    todo = list(pairs)

    def early():
        if todo:
            c, first = todo.pop(0)
            a, b = sides(high, c, first, half), sides(low, c, first, half)
            mixed = dot_nn(twice, jnp.concatenate([a, b], axis=0)) + dot_nn(first_rows[half:], a)
            put(c, first, 0, mixed)
            if first + 2 == cells_x:
                send((c, pl.ds(0, snaps // 2)), out_sem.at[0, c])

    for home in range(2, 4):
        work.sweep(home, early)
    while todo:
        early()
    second_rows = blocks(work.rows_of((2, 3)), size)
    for n, (c, first) in enumerate(pairs):
        mixed = dot_nn(second_rows, sides(high, c, first, size))
        mixed = mixed[:half] + mixed[half:]
        mixed += dot_nn(second_rows[:half], sides(low, c, first, size))
        put(c, first, snaps // 2, mixed)
        send((c, pl.ds(snaps // 2, snaps // 2), pl.ds(first, 2)), out_sem.at[1, n])
    for copy in stores:
        copy.wait()


def mix_call(shape, gram, unscale, high, low):
    return pl.pallas_call(
        mix_kernel,
        out_shape=jax.ShapeDtypeStruct(shape, F32),
        in_specs=[pl.BlockSpec(memory_space=pltpu.VMEM)] * 4,
        out_specs=pl.BlockSpec(memory_space=pltpu.HBM),
        scratch_shapes=[
            pltpu.VMEM(shape, F32),
            pltpu.SemaphoreType.DMA((2, 3 * shape[2] // 2)),
        ],
        compiler_params=pltpu.CompilerParams(vmem_limit_bytes=28 << 20),
        name="mix",
    )(gram, unscale, high, low)


def solution(mesh):
    placed = (P(None, None, "gx", "gz", None), P("gx", "gz", None))
    axes = (mesh.shape["gx"], mesh.shape["gz"])

    def per_device(velocity, weights):
        rows_all = 3 * weights.size * axes[0] * axes[1]
        scale = float(rows_all) ** 0.5
        velocity, weights = (
            pltpu.with_memory_space_constraint(a, pltpu.HBM) for a in (velocity, weights)
        )
        gram, high, low, unscale = gram_call(axes, scale, velocity, weights)
        return mix_call(velocity.shape, gram, unscale, high, low)

    return jax.shard_map(
        per_device,
        mesh=mesh,
        in_specs=placed,
        out_specs=P(None, None, "gx", "gz", None),
        check_vma=False,
    )
```
